256 devices in a mesh: grp: 2 (over x_hi), seq: 64 (over y, z, core), head: 2 (over x_lo).
Axes of the slice: x: 4 (x_hi: 2, x_lo: 2; x = x_hi * 2 + x_lo), y: 4, z: 8, core: 2. Of those that a mesh axis runs over, the one named last changes fastest.
Arguments:
- patches: bfloat16 [24576, 1280], P(('grp', 'seq')), parts along dimension 0, may hold values from -6 to 6
- ln_gain: float32 [1280], replicated, may hold values from 0.25 to 1.75
- ln_bias: float32 [1280], replicated, may hold values from -3 to 3
- qkv_weight: bfloat16 [1280, 3, 1280], P(None, None, 'head'), may hold values from -0.15625 to 0.15625
- proj_weight: bfloat16 [1280, 1280], P('head'), may hold values from -0.15625 to 0.15625
- proj_bias: float32 [1280], replicated, may hold values from -3 to 3
- merge_gain: float32 [1280], replicated, may hold values from 0.25 to 1.75
- merge_bias: float32 [1280], replicated, may hold values from -3 to 3
- visual_kv_weight: bfloat16 [5120, 2, 512], P(None, None, 'head'), may hold values from -0.078125 to 0.078125
- image_tokens: int32 [256], P('grp'), parts along dimension 0, may hold values from 2 to 47, as said below
- text_before: int32 [256], P('grp'), parts along dimension 0, may hold values from 0 to 8192, as said below
- text_order: int32 [16384], P(('grp', 'seq')), parts along dimension 0, may hold values from 0 to 8191, each once
- queries: bfloat16 [16384, 4096], P(('grp', 'seq'), 'head'), parts along dimension 0, may hold values from -44 to 44
- text_kv: bfloat16 [16384, 2, 512], P(('grp', 'seq'), None, 'head'), parts along dimension 0, may hold values from -4 to 4
Outputs:
- attended: bfloat16 [16384, 4096], P(('grp', 'seq'), 'head'), parts along dimension 0
- visual_kv: bfloat16 [6144, 2, 512], P(('grp', 'seq'), None, 'head'), parts along dimension 0
The draws below stay inside these ranges and needn't reach their ends.
There are 2 independent parts, one for each index of `grp`. The reference program is written for one: setup_inputs(seed, part) draws one part's arguments, and reference() takes and returns one part's arrays. A program takes and returns all parts, laid end to end along the dimension named above; an argument that names none is the same for every part. Nothing has to cross between parts.
Inputs may be any that keep to these rules, and one draw needn't show every extreme that they name: `image_tokens`: they sum to 3072; each run of 48 visual tokens of one index of seq holds the last token of exactly two images (the last index: of one image and of the last image), so an image crosses every boundary between indices; the last image holds 47 tokens. `text_before`: non-decreasing. `text_order`: each number once.
All inputs are finite; a program needn't handle non-finite values.
Results may differ from the reference program's by a relative error of at most 0.0095.
Values may be sent and summed in bfloat16 or wider, within the bound.
A program may use at most 128 MiB of HBM per device.

```python
import math
import jax
import jax.numpy as jnp
from jax import lax

VIT_D = 1280
VIT_HEADS = 16
VIT_HD = 80
HEAD_DIM = 128
GROUP = 8
KV_HEADS = 4
PATCH_DEV = 192
TOK_DEV = 128
VT_DEV = 48
MERGED = 5120
KVW = 512
QW = 4096
IMAGES = 128
PATCHES = 12288
VIS = 3072
TOKENS = 8192
N_SEQ = 64


def shared_keys(key):
    drawn = jax.random.normal(jax.random.fold_in(key, 11), (TOKENS, KV_HEADS, HEAD_DIM), jnp.float32)
    return jnp.clip(drawn, -4.0, 4.0)


def draw_queries(key, part):
    drawn_draw = jax.random.normal(jax.random.fold_in(key, 12), (TOKENS, KV_HEADS, GROUP, HEAD_DIM), jnp.float32)
    drawn_draw = jnp.clip(drawn_draw, -4.0, 4.0)
    return drawn_draw.reshape(TOKENS, QW).astype(jnp.bfloat16)


def draw_text_kv(key, part):
    keys_drawn = shared_keys(key).reshape(TOKENS, KVW)
    values_drawn = jnp.clip(jax.random.normal(jax.random.fold_in(key, 14), (TOKENS, KVW), jnp.float32), -4.0, 4.0)
    return jnp.stack([keys_drawn, values_drawn], axis=1).astype(jnp.bfloat16)


def draw_text_before(key, part):
    drawn = jax.random.randint(jax.random.fold_in(key, 15), (IMAGES,), 0, TOKENS + 1)
    return jnp.sort(drawn).astype(jnp.int32)


def draw_image_tokens(key, part):
    quarter = VT_DEV // 4
    device_starts = jnp.arange(N_SEQ, dtype=jnp.int32) * VT_DEV
    early_cuts = jax.random.randint(jax.random.fold_in(key, 21), (N_SEQ,), 2, quarter + 2).astype(jnp.int32) + device_starts
    early_cuts = early_cuts.at[N_SEQ - 1].set((N_SEQ - 1) * VT_DEV + 1)
    late_cuts = jax.random.randint(jax.random.fold_in(key, 22), (N_SEQ - 1,), VT_DEV - quarter, VT_DEV).astype(jnp.int32) + device_starts[:-1]
    paired = jnp.stack([early_cuts[:-1], late_cuts], axis=1).reshape(2 * N_SEQ - 2)
    image_ends = jnp.concatenate([paired, early_cuts[N_SEQ - 1:], jnp.full((1,), VIS, jnp.int32)])
    image_starts = jnp.concatenate([jnp.zeros((1,), jnp.int32), image_ends[:-1]])
    return (image_ends - image_starts).astype(jnp.int32)


def steps_of(own_key, shape, pieces, least, top_value):
    level, own = 1.0, jax.random.fold_in(own_key, 6)
    for dim, blocks in pieces:
        draws = jnp.exp(jax.random.uniform(jax.random.fold_in(own, dim), (blocks,), jnp.float32, least / len(pieces), top_value / len(pieces)))
        level = level * jnp.repeat(draws, shape[dim] // blocks).reshape([-1 if axis == dim else 1 for axis in range(len(shape))])
    return level


def noise(stream_key, shape, scale, limit, split=(), kind=jnp.bfloat16):
    values = scale * jax.random.normal(stream_key, shape, jnp.float32)
    if split:
        values = values * steps_of(stream_key, shape, split, -0.22, 0.18)
    return jnp.clip(values, -limit, limit).astype(kind)


def setup_inputs(seed: int = 0, part: int = 0) -> dict:
    splits = jax.random.split(jax.random.key(seed), 15)
    own_keys = jax.random.split(jax.random.fold_in(splits[14], part), 15)
    patches = noise(own_keys[0], (PATCHES, VIT_D), 1.0, 6.0, ((0, 64),))
    ln_gain = jnp.clip(1.0 + 0.15 * jax.random.normal(splits[1], (VIT_D,), jnp.float32), 0.25, 1.75)
    ln_bias = noise(splits[2], (VIT_D,), 0.5, 3.0, (), jnp.float32)
    qkv_weight = noise(splits[3], (VIT_D, 3, VIT_D), VIT_D ** -0.5, 0.15625, ((2, 2),))
    proj_weight = noise(splits[4], (VIT_D, VIT_D), VIT_D ** -0.5, 0.15625, ((0, 2),))
    proj_bias = noise(splits[5], (VIT_D,), 0.5, 3.0, (), jnp.float32)
    merge_gain = jnp.clip(1.0 + 0.15 * jax.random.normal(splits[6], (VIT_D,), jnp.float32), 0.25, 1.75)
    merge_bias = noise(splits[7], (VIT_D,), 0.5, 3.0, (), jnp.float32)
    visual_kv_weight = noise(splits[8], (MERGED, 2, KVW), MERGED ** -0.5, 0.078125, ((2, 2),))
    image_tokens = draw_image_tokens(jax.random.fold_in(jax.random.fold_in(splits[14], part), 71), part)
    text_before = draw_text_before(jax.random.fold_in(jax.random.fold_in(splits[14], part), 71), part)
    text_order = jax.random.permutation(own_keys[11], TOKENS).astype(jnp.int32)
    queries = draw_queries(jax.random.fold_in(jax.random.fold_in(splits[14], part), 71), part)
    text_kv = draw_text_kv(jax.random.fold_in(jax.random.fold_in(splits[14], part), 71), part)
    return dict(patches=patches, ln_gain=ln_gain, ln_bias=ln_bias, qkv_weight=qkv_weight, proj_weight=proj_weight, proj_bias=proj_bias, merge_gain=merge_gain, merge_bias=merge_bias, visual_kv_weight=visual_kv_weight, image_tokens=image_tokens, text_before=text_before, text_order=text_order, queries=queries, text_kv=text_kv)


epsilon = 1e-06
masked_score = -1e+30

def layer_norm(inputs, scale_gain, shift_bias):
    centre = lax.optimization_barrier(jnp.mean(inputs, axis=-1, keepdims=True))
    centred = inputs - centre
    spread = lax.optimization_barrier(jnp.mean(centred * centred, axis=-1, keepdims=True))
    return centred * lax.rsqrt(spread + epsilon) * scale_gain + shift_bias

def reference(patches, ln_gain, ln_bias, qkv_weight, proj_weight, proj_bias, merge_gain, merge_bias, visual_kv_weight, image_tokens, text_before, text_order, queries, text_kv):
    normed = layer_norm(patches.astype(jnp.float32), ln_gain, ln_bias).astype(jnp.bfloat16)
    projected = jnp.dot(normed, qkv_weight.reshape(VIT_D, 3 * VIT_D), preferred_element_type=jnp.float32).astype(jnp.bfloat16)
    projected = projected.reshape(PATCHES, 3, VIT_HEADS, VIT_HD)
    image_ends = 4 * jnp.cumsum(image_tokens)
    patch_index = jnp.arange(PATCHES, dtype=jnp.int32)
    image_id = lax.optimization_barrier(jnp.sum((patch_index[:, None] >= image_ends[None, :]).astype(jnp.int32), axis=1))
    padded_kv = jnp.pad(projected[:, 1:], ((PATCH_DEV, PATCH_DEV), (0, 0), (0, 0), (0, 0)))
    padded_ids = jnp.pad(image_id, (PATCH_DEV, PATCH_DEV), constant_values=-1)

    def vit_block(block_index):
        first_row = block_index * PATCH_DEV
        block_query = lax.dynamic_slice_in_dim(projected[:, 0], first_row, PATCH_DEV, 0).astype(jnp.float32)
        block_kv = lax.dynamic_slice_in_dim(padded_kv, first_row, 3 * PATCH_DEV, 0).astype(jnp.float32)
        query_ids = lax.dynamic_slice_in_dim(image_id, first_row, PATCH_DEV, 0)
        key_ids = lax.dynamic_slice_in_dim(padded_ids, first_row, 3 * PATCH_DEV, 0)
        scores = jnp.einsum('qhd,khd->hqk', block_query, block_kv[:, 0]) / math.sqrt(VIT_HD)
        allowed = query_ids[:, None] == key_ids[None, :]
        scores = jnp.where(allowed[None], scores, masked_score)
        weights = jax.nn.softmax(scores, axis=-1)
        rounded = lax.optimization_barrier(weights.astype(jnp.bfloat16)).astype(jnp.float32)
        mixed_rows = jnp.einsum('hqk,khd->qhd', rounded, block_kv[:, 1])
        return mixed_rows.astype(jnp.bfloat16).reshape(PATCH_DEV, VIT_D)
    vit_mixed = lax.map(vit_block, jnp.arange(N_SEQ, dtype=jnp.int32)).reshape(PATCHES, VIT_D)
    encoded = patches.astype(jnp.float32) + jnp.dot(vit_mixed, proj_weight, preferred_element_type=jnp.float32) + proj_bias
    encoded = encoded.astype(jnp.bfloat16)
    merged = layer_norm(encoded.astype(jnp.float32), merge_gain, merge_bias).astype(jnp.bfloat16).reshape(VIS, MERGED)
    visual_kv = jnp.dot(merged, visual_kv_weight.reshape(MERGED, 2 * KVW), preferred_element_type=jnp.float32)
    visual_kv = visual_kv.astype(jnp.bfloat16).reshape(VIS, 2, KVW)
    text_pos = text_order + lax.optimization_barrier(jnp.sum(jnp.where(text_before[None, :] <= text_order[:, None], image_tokens[None, :], 0), axis=1))
    image_starts = jnp.cumsum(image_tokens) - image_tokens
    steps_before = text_before - jnp.concatenate([jnp.zeros((1,), jnp.int32), text_before[:-1]])
    visual_index = jnp.arange(VIS, dtype=jnp.int32)
    vis_pos = visual_index + lax.optimization_barrier(jnp.sum(jnp.where(image_starts[None, :] <= visual_index[:, None], steps_before[None, :], 0), axis=1))
    all_kv = jnp.concatenate([text_kv, visual_kv], axis=0)
    all_pos = jnp.concatenate([text_pos, vis_pos])

    def llm_block(block_index):
        row_block = block_index // KV_HEADS
        kv_head = block_index % KV_HEADS
        block_query = lax.dynamic_slice_in_dim(queries, row_block * TOK_DEV, TOK_DEV, 0)
        block_query = lax.dynamic_slice_in_dim(block_query, kv_head * GROUP * HEAD_DIM, GROUP * HEAD_DIM, 1)
        block_query = block_query.astype(jnp.float32).reshape(TOK_DEV, GROUP, HEAD_DIM)
        query_pos = lax.dynamic_slice_in_dim(text_pos, row_block * TOK_DEV, TOK_DEV, 0)
        head_keys = lax.dynamic_slice_in_dim(all_kv[:, 0], kv_head * HEAD_DIM, HEAD_DIM, 1).astype(jnp.float32)
        head_values = lax.dynamic_slice_in_dim(all_kv[:, 1], kv_head * HEAD_DIM, HEAD_DIM, 1).astype(jnp.float32)
        scores = jnp.einsum('qgd,kd->qgk', block_query, head_keys) / math.sqrt(HEAD_DIM)
        allowed = (all_pos[None, :] <= query_pos[:, None])[:, None, :]
        scores = jnp.where(allowed, scores, masked_score)
        row_max = lax.optimization_barrier(jnp.max(scores, axis=-1, keepdims=True))
        weights = jnp.where(allowed, jnp.exp(scores - row_max), 0.0)
        row_sum = lax.optimization_barrier(jnp.sum(weights, axis=-1))
        rounded = lax.optimization_barrier(weights.astype(jnp.bfloat16)).astype(jnp.float32)
        summed = jnp.einsum('qgk,kd->qgd', rounded, head_values)
        return (summed / row_sum[..., None]).reshape(TOK_DEV, GROUP * HEAD_DIM)
    outputs = lax.map(llm_block, jnp.arange(N_SEQ * KV_HEADS, dtype=jnp.int32))
    outputs = outputs.reshape(N_SEQ, KV_HEADS, TOK_DEV, GROUP * HEAD_DIM)
    attended = jnp.transpose(outputs, (0, 2, 1, 3)).reshape(TOKENS, QW)
    return (attended.astype(jnp.bfloat16), visual_kv)
```

```python
import functools
import heapq
import math

import jax
import jax.numpy as jnp
from jax import lax
from jax.experimental import pallas as pl
from jax.experimental.pallas import tpu as pltpu
from jax.sharding import Mesh
from jax.sharding import PartitionSpec as P

MESH = pl.DeviceIdType.MESH


VIT_HD = 80
HEAD_DIM = 128
GROUP = 8
SEQ = ("seq_0", "seq_1", "seq_2")
GRP_SEQ = ("grp", "seq_0", "seq_1", "seq_2")


NEG = -1e30
C=math.log2(math.e)/math.sqrt(128)
G=8; D=128
BIG=2**30

def attend_kernel(q_ref, kvt_ref, kvv_ref, qpos_ref, kp_ref, perm_ref, out_ref,
                  kbuf, vbuf, s_sc, x_sc, p_sc, a_sc, o_sc, m_sc, l_sc, srt_sc, sem, *, TQ, NT, NV):
    R=G*TQ
    nq=128//TQ
    KB=1024
    S=kvt_ref.shape[0]
    RB=KB//S
    def copies(h,b):
        out=[]
        for j,buf in ((0,kbuf),(1,vbuf)):
            c=j*256+h*D
            if b<NT:
                src=kvt_ref.at[:,b*RB:(b+1)*RB,c:c+D]
                dst=buf.at[h,b]
            else:
                src=kvv_ref.at[b-NT,:,:,c:c+D]
                dst=buf.at[h,b]
            out.append(pltpu.make_async_copy(src,dst,sem.at[h,b]))
        return out
    for h in range(2):
        for b in range(NT+NV):
            for c in copies(h,b): c.start()
    kmin=jnp.min(kp_ref[...],axis=1,keepdims=True)
    tmin=kmin[0:NT]; vmin=kmin[NT:NT+NV]
    for h in range(2):
        for b in range(NT+NV):
            for c in copies(h,b): c.wait()
        for i in range(nq):
            qp=qpos_ref[i*TQ:(i+1)*TQ,0:1]
            qhi=jnp.max(qp,axis=0,keepdims=True)
            nt=jnp.sum((tmin<=qhi).astype(jnp.int32))
            nv=jnp.sum((vmin<=qhi).astype(jnp.int32))
            n=nt+nv
            q=jnp.concatenate([q_ref[i*TQ:(i+1)*TQ,(h*G+g)*D:(h*G+g+1)*D] for g in range(G)],axis=0)
            def blk(j):
                return jnp.minimum(jnp.where(j<nt,j,j-nt+NT),NT+NV-1)
            def pblk(j):
                return jnp.where(j<n,blk(j),NT+NV)
            def qk(j,t):
                k=kbuf[h,blk(j)].reshape(KB,D)
                s=lax.dot_general(q,k,(((1,),(1,)),((),())),preferred_element_type=jnp.float32)
                bias=jnp.where(kp_ref[pl.ds(pblk(j),1),:]<=qp,0.0,NEG)
                s=s+jnp.concatenate([bias]*G,axis=0)
                s_sc[t]=s
                x=s[:,0:128]
                for c in range(1,KB//128): x=jnp.maximum(x,s[:,c*128:(c+1)*128])
                x_sc[t]=x
            def soft(t):
                m_old=m_sc[:,0:1]
                m_new=jnp.maximum(m_old,jnp.max(x_sc[t],axis=1,keepdims=True))
                mc=m_new*C
                p=jnp.exp2(s_sc[t]*C-mc)
                a=jnp.exp2(m_old*C-mc)
                l=p[:,0:128]
                for c in range(1,KB//128): l=l+p[:,c*128:(c+1)*128]
                l_sc[...]=l_sc[...]*a+l
                p_sc[t]=p.astype(jnp.bfloat16)
                a_sc[t]=jnp.broadcast_to(a,(R,128))
                m_sc[...]=jnp.broadcast_to(m_new,m_sc.shape)
            def pv(j,t):
                v=vbuf[h,blk(jnp.maximum(j,0))].reshape(KB,D)
                o_sc[...]=o_sc[...]*a_sc[t]+jnp.dot(p_sc[t],v,preferred_element_type=jnp.float32)
            m_sc[...]=jnp.full_like(m_sc,NEG)
            l_sc[...]=jnp.zeros_like(l_sc)
            o_sc[...]=jnp.zeros_like(o_sc)
            p_sc[1]=jnp.zeros_like(p_sc[1])
            a_sc[1]=jnp.zeros_like(a_sc[1])
            qk(0,0)
            @pl.loop(0,(n+1)//2)
            def _(jj):
                j=jj*2
                pv(j-1,1); qk(j+1,1); soft(0)
                pv(j,0); qk(j+2,0); soft(1)
            pv(((n+1)//2)*2-1,1)
            o=(o_sc[...]/jnp.sum(l_sc[...],axis=1,keepdims=True)).astype(jnp.bfloat16)
            for g in range(G):
                srt_sc[i*TQ:(i+1)*TQ,g*D:(g+1)*D]=o[g*TQ:(g+1)*TQ]
        out_ref[:,h*1024:(h+1)*1024]=jnp.dot(perm_ref[...],srt_sc[...],preferred_element_type=jnp.float32).astype(jnp.bfloat16)

def attend(q,kvt,kvv,qpos,kp,perm):
    S=kvt.shape[0]; V=kvv.shape[0]*kvv.shape[1]
    KB=1024; RB=KB//S; NT=S*128//KB; NV=V//KB
    kvv4=kvv.reshape(NV,S,RB,512)
    TQ=32
    R=G*TQ
    vm=lambda: pl.BlockSpec(memory_space=pltpu.VMEM)
    hb=lambda: pl.BlockSpec(memory_space=pl.ANY)
    return pl.pallas_call(
        functools.partial(attend_kernel,TQ=TQ,NT=NT,NV=NV),
        in_specs=[vm(),hb(),hb(),vm(),vm(),vm()],
        out_specs=vm(),
        out_shape=jax.ShapeDtypeStruct((128,2048),jnp.bfloat16),
        scratch_shapes=[pltpu.VMEM((2,NT+NV,S,RB,D),jnp.bfloat16),pltpu.VMEM((2,NT+NV,S,RB,D),jnp.bfloat16),
          pltpu.VMEM((2,R,KB),jnp.float32),pltpu.VMEM((2,R,128),jnp.float32),pltpu.VMEM((2,R,KB),jnp.bfloat16),pltpu.VMEM((2,R,128),jnp.float32),
          pltpu.VMEM((R,128),jnp.float32),pltpu.VMEM((R,128),jnp.float32),pltpu.VMEM((R,128),jnp.float32),pltpu.VMEM((128,1024),jnp.bfloat16),
          pltpu.SemaphoreType.DMA((2,NT+NV))],
        compiler_params=pltpu.CompilerParams(vmem_limit_bytes=60<<20),
        name="attend",
    )(q,kvt,kvv4,qpos,kp,perm)


def ring_plan(na, nb):
    free = {}
    heap = []
    count = [0]
    def send(axis, way, a, b, part, at):
        start = max(at, free.get((axis, way), 0.0))
        end = start + (1.0 if part == 0 else 0.5)
        free[(axis, way)] = end
        count[0] += 1
        heapq.heappush(heap, (end + 0.9, count[0], axis, way, a, b, part))
    def spread(axis, size, way, off, at, a, b):
        nxt = off + 1
        if nxt < size // 2:
            part = 0
        elif nxt == size // 2:
            part = 1 if way == 1 else 2
        else:
            return None
        return part
    def go(axis, size, way, off, at, a, b):
        part = spread(axis, size, way, off, at, a, b)
        if part is not None:
            na_, nb_ = (a + way, b) if axis == "a" else (a, b + way)
            send(axis, way, na_, nb_, part, at)
    for way in (1, -1):
        go("a", na, way, 0, 0.0, 0, 0)
    for way in (1, -1):
        go("b", nb, way, 0, 0.0, 0, 0)
    order = []
    halves = {}
    while heap:
        at, _, axis, way, a, b, part = heapq.heappop(heap)
        order.append((axis, way, a, b, part))
        if axis == "a":
            if part == 0:
                go("a", na, way, abs(a), at, a, b)
                for w in (1, -1):
                    go("b", nb, w, 0, at, a, b)
            else:
                key = abs(a)
                halves[("a", key, b)] = halves.get(("a", key, b), 0) + 1
                if halves[("a", key, b)] == 2:
                    for w in (1, -1):
                        go("b", nb, w, 0, at, na // 2, b)
        else:
            if part == 0:
                go("b", nb, way, abs(b), at, a, b)
    return order

class Gather:
    def __init__(self, own, out, rows, cut, send_sem, recv_sem, ny=4, nz=8):
        self.own, self.out, self.rows, self.cut = own, out, rows, cut
        self.send_sem, self.recv_sem = send_sem, recv_sem
        self.ny, self.nz = ny, nz
        self.y, self.z, self.c = lax.axis_index("seq_0"), lax.axis_index("seq_1"), lax.axis_index("seq_2")
        self.sent = []
        self.plans = [ring_plan(nz, ny), ring_plan(ny, nz)]
    def sid(self, c, a, b):
        dz, dy = (a, b) if c == 0 else (b, a)
        y = lax.rem(self.y - dy + self.ny, self.ny)
        z = lax.rem(self.z - dz + self.nz, self.nz)
        return (y * self.nz + z) * 2 + c
    def part(self, ref, part):
        if part == 0: return ref
        return ref.at[0:self.cut] if part == 1 else ref.at[self.cut:self.rows]
    def desc(self, src, s, part, n, dev):
        return pltpu.make_async_remote_copy(
            src_ref=self.part(src, part), dst_ref=self.part(self.out.at[s], part),
            send_sem=self.send_sem.at[n], recv_sem=self.recv_sem.at[s, 1 if part == 2 else 0],
            device_id=dev, device_id_type=MESH)
    def neighbour(self, c, axis, way):
        along_z = (axis == "a") == (c == 0)
        if along_z:
            return {"seq_1": lax.rem(self.z + way + self.nz, self.nz)}
        return {"seq_0": lax.rem(self.y + way + self.ny, self.ny)}
    def start(self, c, src, s, part, dev):
        d = self.desc(src, s, part, len(self.sent), dev)
        d.start()
        self.sent.append(d)
    def wait(self, s, part):
        self.desc(self.out.at[s], s, part, 0, {"seq_2": 1 - self.c}).wait_recv()
    def to_partner(self, src, s):
        self.start(None, src, s, 0, {"seq_2": 1 - self.c})
    def begin(self, c):
        self.sent = []
        s = self.sid(c, 0, 0)
        for axis in ("a", "b"):
            for way in (1, -1):
                self.start(c, self.own, s, 0, self.neighbour(c, axis, way))
        self.to_partner(self.own, s)
    def events(self, c):
        na, nb = (self.nz, self.ny) if c == 0 else (self.ny, self.nz)
        steps = []
        halves = {}
        def step(axis, way, a, b, part):
            s = self.sid(c, a, b)
            self.wait(s, part)
            src = self.out.at[s]
            size = na if axis == "a" else nb
            off = abs(a) if axis == "a" else abs(b)
            if part == 0:
                nxt = off + 1
                if nxt < size // 2: p = 0
                else: p = 1 if way == 1 else 2
                self.start(c, src, s, p, self.neighbour(c, axis, way))
                done = True
            else:
                key = (axis, off, abs(a) if abs(a)*2==na else a)
                halves[key] = halves.get(key, 0) + 1
                done = halves[key] == 2
            if done:
                if axis == "a":
                    for w in (1, -1):
                        self.start(c, src, s, 0, self.neighbour(c, "b", w))
                self.to_partner(src, s)
        for e in self.plans[c]:
            steps.append(functools.partial(step, *e))
        return steps
    def finish(self, c):
        na, nb = (self.nz, self.ny) if c == 0 else (self.ny, self.nz)
        for a in range(na):
            for b in range(nb):
                self.wait(self.sid(1 - c, a, b) if False else self.other(c, a, b), 0)
        for d in self.sent:
            d.wait_send()
    def other(self, c, a, b):
        return self.sid(1 - c, *((b, a)))

def barrier(peers_fn):
    sem = pltpu.get_barrier_semaphore()
    y, z, c = lax.axis_index("seq_0"), lax.axis_index("seq_1"), lax.axis_index("seq_2")
    n = 0
    for dev in peers_fn(y, z, c):
        pl.semaphore_signal(sem, inc=1, device_id=dev, device_id_type=MESH); n += 1
    pl.semaphore_wait(sem, n)

def near(y, z, c, ny=4, nz=8):
    return [{"seq_0": lax.rem(y + 1, ny)}, {"seq_0": lax.rem(y + ny - 1, ny)},
            {"seq_1": lax.rem(z + 1, nz)}, {"seq_1": lax.rem(z + nz - 1, nz)}, {"seq_2": 1 - c}]


def gather_kernel(text_ref, vis_ref, text_out, vis_out, ts, tr, vs, vr, loc_sem, *, ny, nz):
    barrier(functools.partial(near, ny=ny, nz=nz))
    core = lax.axis_index("seq_2")
    me = (lax.axis_index("seq_0") * nz + lax.axis_index("seq_1")) * 2 + core
    locs = [pltpu.make_async_copy(text_ref, text_out.at[me], loc_sem.at[0]),
            pltpu.make_async_copy(vis_ref, vis_out.at[me], loc_sem.at[1])]
    for loc in locs:
        loc.start()
    for c in (0, 1):
        @pl.when(core == c)
        def _():
            v = Gather(vis_ref, vis_out, vis_ref.shape[0], vis_ref.shape[0] // 2, vs, vr, ny, nz)
            t = Gather(text_ref, text_out, text_ref.shape[0], 64, ts, tr, ny, nz)
            v.begin(c)
            t.begin(c)
            for a, b in zip(v.events(c), t.events(c)):
                a()
                b()
            v.finish(c)
            t.finish(c)
    for loc in locs:
        loc.wait()


def gather(text, vis, ny, nz):
    n = ny * nz * 2
    any_space = pl.BlockSpec(memory_space=pl.ANY)
    in_vmem = pl.BlockSpec(memory_space=pltpu.VMEM)
    dma = pltpu.SemaphoreType.DMA
    return pl.pallas_call(
        functools.partial(gather_kernel, ny=ny, nz=nz),
        in_specs=[in_vmem, in_vmem],
        out_specs=[any_space, any_space],
        out_shape=[jax.ShapeDtypeStruct((n, *x.shape), x.dtype) for x in (text, vis)],
        scratch_shapes=[dma((2 * n + 16,)), dma((n, 2)), dma((2 * n + 16,)), dma((n, 2)), dma((2,))],
        compiler_params=pltpu.CompilerParams(collective_id=1, has_side_effects=True),
        name="gather",
    )(text, vis)


epsilon = 1e-06
masked_score = -1e30


def extended(cells, sides, width):
    for axis, dim in sides:
        count = lax.axis_size(axis)
        ends = count - 1
        head = lax.slice_in_dim(cells, 0, width, axis=dim)
        tail = lax.slice_in_dim(cells, cells.shape[dim] - width, cells.shape[dim], axis=dim)
        cells = jnp.concatenate(
            [
                lax.ppermute(tail, axis, [(i, (i + 1) % count) for i in range(ends)]),
                cells,
                lax.ppermute(head, axis, [((i + 1) % count, i) for i in range(ends)]),
            ],
            axis=dim,
        )
    return cells


def sent_to_all(shard, axis):
    size = lax.axis_size(axis)
    return lax.all_to_all(
        jnp.broadcast_to(shard[None], (size, *shard.shape)), axis, 0, 0, tiled=True
    )


def of_everyone(shard, axis):
    return sent_to_all(shard, axis).astype(jnp.float32).sum(axis=0)


def layer_norm(inputs, scale_gain, shift_bias):
    centre = jnp.mean(inputs, axis=-1, keepdims=True)
    centred = inputs - centre
    spread = jnp.mean(centred * centred, axis=-1, keepdims=True)
    return centred * lax.rsqrt(spread + epsilon) * scale_gain + shift_bias


def per_device(
    patches,
    ln_gain,
    ln_bias,
    qkv_weight,
    proj_weight,
    proj_bias,
    merge_gain,
    merge_bias,
    visual_kv_weight,
    image_tokens,
    text_before,
    text_order,
    queries,
    text_kv,
):
    seq_index = lax.axis_index(SEQ)
    patch_rows = patches.shape[0]
    model_width = patches.shape[1]
    merged_rows = patch_rows // 4
    head_cols = qkv_weight.shape[2]
    local_heads = head_cols // VIT_HD
    normed = layer_norm(patches.astype(jnp.float32), ln_gain, ln_bias).astype(jnp.bfloat16)
    projected = jnp.dot(
        normed, qkv_weight.reshape(model_width, 3 * head_cols), preferred_element_type=jnp.float32
    )
    projected = projected.astype(jnp.bfloat16).reshape(patch_rows, 3, head_cols)
    near_kv = extended(projected[:, 1:], ((SEQ, 0),), patch_rows)
    total_patches = patch_rows * lax.axis_size(SEQ)
    image_ends = 4 * jnp.cumsum(image_tokens)
    near_index = seq_index * patch_rows - patch_rows + jnp.arange(3 * patch_rows, dtype=jnp.int32)
    near_ids = jnp.sum((near_index[:, None] >= image_ends[None, :]).astype(jnp.int32), axis=1)
    near_ids = jnp.where((near_index >= 0) & (near_index < total_patches), near_ids, -1)
    own_ids = near_ids[patch_rows : 2 * patch_rows]
    queries_vit = projected[:, 0].reshape(patch_rows, local_heads, VIT_HD)
    near_keys = near_kv[:, 0].reshape(3 * patch_rows, local_heads, VIT_HD)
    near_values = near_kv[:, 1].reshape(3 * patch_rows, local_heads, VIT_HD)
    scores = jnp.einsum(
        "qhd,khd->hqk", queries_vit, near_keys, preferred_element_type=jnp.float32
    ) / math.sqrt(VIT_HD)
    allowed = own_ids[:, None] == near_ids[None, :]
    scores = jnp.where(allowed[None], scores, masked_score)
    weights = jax.nn.softmax(scores, axis=-1).astype(jnp.bfloat16)
    vit_mixed = jnp.einsum("hqk,khd->qhd", weights, near_values, preferred_element_type=jnp.float32)
    vit_mixed = vit_mixed.astype(jnp.bfloat16).reshape(patch_rows, head_cols)
    partial_value = jnp.dot(vit_mixed, proj_weight, preferred_element_type=jnp.float32)
    summed = of_everyone(partial_value.astype(jnp.bfloat16), "head").astype(jnp.float32)
    encoded = (patches.astype(jnp.float32) + summed + proj_bias).astype(jnp.bfloat16)
    merged = layer_norm(encoded.astype(jnp.float32), merge_gain, merge_bias).astype(jnp.bfloat16)
    merged = merged.reshape(merged_rows, 4 * model_width)
    visual_kv = jnp.dot(
        merged, visual_kv_weight.reshape(4 * model_width, -1), preferred_element_type=jnp.float32
    )
    visual_kv = visual_kv.astype(jnp.bfloat16).reshape(merged_rows, 2, -1)
    text_pos = text_order + jnp.sum(
        jnp.where(text_before[None, :] <= text_order[:, None], image_tokens[None, :], 0), axis=1
    )
    image_starts = jnp.cumsum(image_tokens) - image_tokens
    steps_before = text_before - jnp.concatenate([jnp.zeros((1,), jnp.int32), text_before[:-1]])

    tokens = queries.shape[0]
    ny, nz = lax.axis_size("seq_0"), lax.axis_size("seq_1")
    rank = jnp.sum((text_order[None, :] < text_order[:, None]).astype(jnp.int32), axis=1)
    hot = (rank[None, :] == jnp.arange(tokens, dtype=jnp.int32)[:, None]).astype(jnp.bfloat16)
    q = jnp.dot(hot, queries, preferred_element_type=jnp.float32).astype(jnp.bfloat16)
    places = jnp.stack([text_pos // 128, text_pos % 128]).astype(jnp.bfloat16)
    places = lax.dot_general(places, hot, (((1,), (1,)), ((), ())), preferred_element_type=jnp.float32)
    kv = jnp.dot(hot, text_kv.reshape(tokens, -1), preferred_element_type=jnp.float32).astype(jnp.bfloat16)
    places_rows = jnp.pad(places.astype(jnp.bfloat16), ((0, 6), (0, kv.shape[1] - tokens)))
    all_text, all_vis = gather(jnp.concatenate([kv, places_rows], axis=0), visual_kv.reshape(merged_rows, -1), ny, nz)
    key_pos = all_text[:, tokens : tokens + 2, :tokens].astype(jnp.int32)
    key_pos = key_pos[:, 0] * 128 + key_pos[:, 1]
    sources = key_pos.shape[0]
    blocks = sources * tokens // 1024
    key_pos = key_pos.reshape(sources, blocks, tokens // blocks).transpose(1, 0, 2).reshape(blocks, 1024)
    visual_index = jnp.arange(sources * merged_rows, dtype=jnp.int32)
    all_vis_pos = visual_index + jnp.sum(
        jnp.where(image_starts[None, :] <= visual_index[:, None], steps_before[None, :], 0), axis=1
    )
    kp = jnp.concatenate([key_pos, all_vis_pos.reshape(-1, 1024), jnp.full((1, 1024), BIG, jnp.int32)], axis=0)
    places = places.astype(jnp.int32)
    q_pos = (places[0] * 128 + places[1])[:, None]
    attended = attend(q, all_text, all_vis, q_pos, kp, hot.T)
    return (attended, visual_kv)


def solution(mesh):
    split = Mesh(
        mesh.devices.reshape(mesh.shape["grp"], 4, 8, 2, mesh.shape["head"]),
        ("grp", "seq_0", "seq_1", "seq_2", "head"),
    )
    in_specs = (
        P(GRP_SEQ, None),
        P(),
        P(),
        P(None, None, "head"),
        P("head", None),
        P(),
        P(),
        P(),
        P(None, None, "head"),
        P("grp"),
        P("grp"),
        P(GRP_SEQ),
        P(GRP_SEQ, "head"),
        P(GRP_SEQ, None, "head"),
    )
    out_specs = (P(GRP_SEQ, "head"), P(GRP_SEQ, None, "head"))
    return jax.shard_map(
        per_device, mesh=split, in_specs=in_specs, out_specs=out_specs, check_vma=False
    )
```

```python
import functools
import heapq
import math

import jax
import jax.numpy as jnp
from jax import lax
from jax.experimental import pallas as pl
from jax.experimental.pallas import tpu as pltpu
from jax.sharding import Mesh
from jax.sharding import PartitionSpec as P

MESH = pl.DeviceIdType.MESH


VIT_HD = 80
HEAD_DIM = 128
GROUP = 8
SEQ = ("seq_0", "seq_1", "seq_2")
GRP_SEQ = ("grp", "seq_0", "seq_1", "seq_2")


epsilon = 1e-06
NEG = -1e30
C=math.log2(math.e)/math.sqrt(128)
G=8; D=128
BIG=2**30

def attend_kernel(q_ref, kvt_ref, kvv_ref, qpos_ref, kp_ref, perm_ref, out_ref,
                  kbuf, vbuf, s_sc, x_sc, p_sc, a_sc, o_sc, m_sc, l_sc, srt_sc, sem, *, TQ, NT, NV):
    R=G*TQ
    nq=128//TQ
    KB=1024
    S=kvt_ref.shape[0]
    RB=KB//S
    def copies(h,b):
        out=[]
        for j,buf in ((0,kbuf),(1,vbuf)):
            c=j*256+h*D
            if b<NT:
                src=kvt_ref.at[:,b*RB:(b+1)*RB,c:c+D]
                dst=buf.at[h,b]
            else:
                src=kvv_ref.at[b-NT,:,:,c:c+D]
                dst=buf.at[h,b]
            out.append(pltpu.make_async_copy(src,dst,sem.at[h,b]))
        return out
    for h in range(2):
        for b in range(NT+NV):
            for c in copies(h,b): c.start()
    kmin=jnp.min(kp_ref[...],axis=1,keepdims=True)
    tmin=kmin[0:NT]; vmin=kmin[NT:NT+NV]
    for h in range(2):
        for b in range(NT+NV):
            for c in copies(h,b): c.wait()
        for i in range(nq):
            qp=qpos_ref[i*TQ:(i+1)*TQ,0:1]
            qhi=jnp.max(qp,axis=0,keepdims=True)
            nt=jnp.sum((tmin<=qhi).astype(jnp.int32))
            nv=jnp.sum((vmin<=qhi).astype(jnp.int32))
            n=nt+nv
            q=jnp.concatenate([q_ref[i*TQ:(i+1)*TQ,(h*G+g)*D:(h*G+g+1)*D] for g in range(G)],axis=0)
            def blk(j):
                return jnp.minimum(jnp.where(j<nt,j,j-nt+NT),NT+NV-1)
            def pblk(j):
                return jnp.where(j<n,blk(j),NT+NV)
            def qk(j,t):
                k=kbuf[h,blk(j)].reshape(KB,D)
                s=lax.dot_general(q,k,(((1,),(1,)),((),())),preferred_element_type=jnp.float32)
                bias=jnp.where(kp_ref[pl.ds(pblk(j),1),:]<=qp,0.0,NEG)
                s=s+jnp.concatenate([bias]*G,axis=0)
                s_sc[t]=s
                x=s[:,0:128]
                for c in range(1,KB//128): x=jnp.maximum(x,s[:,c*128:(c+1)*128])
                x_sc[t]=x
            def soft(t):
                m_old=m_sc[:,0:1]
                m_new=jnp.maximum(m_old,jnp.max(x_sc[t],axis=1,keepdims=True))
                mc=m_new*C
                p=jnp.exp2(s_sc[t]*C-mc)
                a=jnp.exp2(m_old*C-mc)
                l=p[:,0:128]
                for c in range(1,KB//128): l=l+p[:,c*128:(c+1)*128]
                l_sc[...]=l_sc[...]*a+l
                p_sc[t]=p.astype(jnp.bfloat16)
                a_sc[t]=jnp.broadcast_to(a,(R,128))
                m_sc[...]=jnp.broadcast_to(m_new,m_sc.shape)
            def pv(j,t):
                v=vbuf[h,blk(jnp.maximum(j,0))].reshape(KB,D)
                o_sc[...]=o_sc[...]*a_sc[t]+jnp.dot(p_sc[t],v,preferred_element_type=jnp.float32)
            m_sc[...]=jnp.full_like(m_sc,NEG)
            l_sc[...]=jnp.zeros_like(l_sc)
            o_sc[...]=jnp.zeros_like(o_sc)
            p_sc[1]=jnp.zeros_like(p_sc[1])
            a_sc[1]=jnp.zeros_like(a_sc[1])
            qk(0,0)
            @pl.loop(0,(n+1)//2)
            def _(jj):
                j=jj*2
                pv(j-1,1); qk(j+1,1); soft(0)
                pv(j,0); qk(j+2,0); soft(1)
            pv(((n+1)//2)*2-1,1)
            o=(o_sc[...]/jnp.sum(l_sc[...],axis=1,keepdims=True)).astype(jnp.bfloat16)
            for g in range(G):
                srt_sc[i*TQ:(i+1)*TQ,g*D:(g+1)*D]=o[g*TQ:(g+1)*TQ]
        out_ref[:,h*1024:(h+1)*1024]=jnp.dot(perm_ref[...],srt_sc[...],preferred_element_type=jnp.float32).astype(jnp.bfloat16)

def attend(q,kvt,kvv,qpos,kp,perm):
    S=kvt.shape[0]; V=kvv.shape[0]*kvv.shape[1]
    KB=1024; RB=KB//S; NT=S*128//KB; NV=V//KB
    kvv4=kvv.reshape(NV,S,RB,512)
    TQ=32
    R=G*TQ
    vm=lambda: pl.BlockSpec(memory_space=pltpu.VMEM)
    hb=lambda: pl.BlockSpec(memory_space=pl.ANY)
    return pl.pallas_call(
        functools.partial(attend_kernel,TQ=TQ,NT=NT,NV=NV),
        in_specs=[vm(),hb(),hb(),vm(),vm(),vm()],
        out_specs=vm(),
        out_shape=jax.ShapeDtypeStruct((128,2048),jnp.bfloat16),
        scratch_shapes=[pltpu.VMEM((2,NT+NV,S,RB,D),jnp.bfloat16),pltpu.VMEM((2,NT+NV,S,RB,D),jnp.bfloat16),
          pltpu.VMEM((2,R,KB),jnp.float32),pltpu.VMEM((2,R,128),jnp.float32),pltpu.VMEM((2,R,KB),jnp.bfloat16),pltpu.VMEM((2,R,128),jnp.float32),
          pltpu.VMEM((R,128),jnp.float32),pltpu.VMEM((R,128),jnp.float32),pltpu.VMEM((R,128),jnp.float32),pltpu.VMEM((128,1024),jnp.bfloat16),
          pltpu.SemaphoreType.DMA((2,NT+NV))],
        compiler_params=pltpu.CompilerParams(vmem_limit_bytes=60<<20),
        name="attend",
    )(q,kvt,kvv4,qpos,kp,perm)


def ring_plan(na, nb):
    free = {}
    heap = []
    count = [0]
    def send(axis, way, a, b, part, at):
        start = max(at, free.get((axis, way), 0.0))
        end = start + (1.0 if part == 0 else 0.5)
        free[(axis, way)] = end
        count[0] += 1
        heapq.heappush(heap, (end + 0.9, count[0], axis, way, a, b, part))
    def spread(axis, size, way, off, at, a, b):
        nxt = off + 1
        if nxt < size // 2:
            part = 0
        elif nxt == size // 2:
            part = 1 if way == 1 else 2
        else:
            return None
        return part
    def go(axis, size, way, off, at, a, b):
        part = spread(axis, size, way, off, at, a, b)
        if part is not None:
            na_, nb_ = (a + way, b) if axis == "a" else (a, b + way)
            send(axis, way, na_, nb_, part, at)
    for way in (1, -1):
        go("a", na, way, 0, 0.0, 0, 0)
    for way in (1, -1):
        go("b", nb, way, 0, 0.0, 0, 0)
    order = []
    halves = {}
    while heap:
        at, _, axis, way, a, b, part = heapq.heappop(heap)
        order.append((axis, way, a, b, part))
        if axis == "a":
            if part == 0:
                go("a", na, way, abs(a), at, a, b)
                for w in (1, -1):
                    go("b", nb, w, 0, at, a, b)
            else:
                key = abs(a)
                halves[("a", key, b)] = halves.get(("a", key, b), 0) + 1
                if halves[("a", key, b)] == 2:
                    for w in (1, -1):
                        go("b", nb, w, 0, at, na // 2, b)
        else:
            if part == 0:
                go("b", nb, way, abs(b), at, a, b)
    return order

def barrier(devices):
    sem = pltpu.get_barrier_semaphore()
    for device in devices:
        pl.semaphore_signal(sem, inc=1, device_id=device, device_id_type=MESH)
    pl.semaphore_wait(sem, len(devices))


def near(y, z, core, ny, nz):
    return [
        {"seq_0": lax.rem(y + 1, ny)},
        {"seq_0": lax.rem(y + ny - 1, ny)},
        {"seq_1": lax.rem(z + 1, nz)},
        {"seq_1": lax.rem(z + nz - 1, nz)},
        {"seq_2": 1 - core},
    ]


class Gather:
    def __init__(self, own, out, cut, send_sem, recv_sem, place, core):
        self.own, self.out, self.rows, self.cut = own, out, own.shape[0], cut
        self.send_sem, self.recv_sem = send_sem, recv_sem
        self.y, self.z, self.ny, self.nz = place
        self.core = core
        self.sizes = (self.nz, self.ny) if core == 0 else (self.ny, self.nz)
        self.plan = ring_plan(*self.sizes)
        self.sent = []
        self.halves = {}
        self.next = 0

    def shard(self, core, dz, dy):
        y = lax.rem(self.y - dy + self.ny, self.ny)
        z = lax.rem(self.z - dz + self.nz, self.nz)
        return (y * self.nz + z) * 2 + core

    def source(self, a, b):
        return self.shard(0, a, b) if self.core == 0 else self.shard(1, b, a)

    def piece(self, ref, part):
        if part == 0:
            return ref
        return ref.at[0 : self.cut] if part == 1 else ref.at[self.cut : self.rows]

    def copy(self, src, index, part, number, device):
        return pltpu.make_async_remote_copy(
            src_ref=self.piece(src, part),
            dst_ref=self.piece(self.out.at[index], part),
            send_sem=self.send_sem.at[number],
            recv_sem=self.recv_sem.at[index, 1 if part == 2 else 0],
            device_id=device,
            device_id_type=MESH,
        )

    def neighbour(self, axis, way):
        if (axis == "a") == (self.core == 0):
            return {"seq_1": lax.rem(self.z + way + self.nz, self.nz)}
        return {"seq_0": lax.rem(self.y + way + self.ny, self.ny)}

    def send(self, src, index, part, device):
        self.copy(src, index, part, len(self.sent), device).start()
        self.sent.append(part)

    def partner(self):
        return {"seq_2": 1 - self.core}

    def begin(self):
        index = self.source(0, 0)
        for axis in ("a", "b"):
            for way in (1, -1):
                self.send(self.own, index, 0, self.neighbour(axis, way))
        self.send(self.own, index, 0, self.partner())

    def wait(self, index, part):
        self.copy(self.own, index, part, 0, self.partner()).wait_recv()

    def step(self, axis, way, a, b, part):
        index = self.source(a, b)
        self.wait(index, part)
        src = self.out.at[index]
        size = self.sizes[0] if axis == "a" else self.sizes[1]
        off = abs(a) if axis == "a" else abs(b)
        done = True
        if part == 0:
            half = 0 if off + 1 < size // 2 else (1 if way == 1 else 2)
            self.send(src, index, half, self.neighbour(axis, way))
        else:
            key = (axis, off, off if axis == "a" else a)
            self.halves[key] = self.halves.get(key, 0) + 1
            done = self.halves[key] == 2
        if done:
            if axis == "a":
                for onward in (1, -1):
                    self.send(src, index, 0, self.neighbour("b", onward))
            self.send(src, index, 0, self.partner())

    def advance(self, count):
        for event in self.plan[self.next : self.next + count]:
            self.step(*event)
        self.next = min(len(self.plan), self.next + count)

    def finish(self):
        self.advance(len(self.plan))
        for dz in range(self.nz):
            for dy in range(self.ny):
                self.wait(self.shard(1 - self.core, dz, dy), 0)
        for number, part in enumerate(self.sent):
            self.copy(self.own, 0, part, number, self.partner()).wait_send()


def norm_rows(x, gain, bias):
    centre = jnp.mean(x, axis=-1, keepdims=True)
    centred = x - centre
    spread = jnp.mean(centred * centred, axis=-1, keepdims=True)
    return centred * lax.rsqrt(spread + epsilon) * gain + bias


def encode_kernel(
    text_ref, patches_ref, norms_ref, own_ids_ref, near_ids_ref, qkv_hbm, proj_hbm, wv_hbm,
    text_out, vis_out, vis_own,
    qkv_w, proj_w, wv, normed, q_sc, keys, values, mixed, part_own, part_far, merged,
    weight_sem, halo_sem, far_sem, ts, tr, vs, vr, loc_sem, *, ny, nz,
):
    f32, bf16 = jnp.float32, jnp.bfloat16
    y, z, core = lax.axis_index("seq_0"), lax.axis_index("seq_1"), lax.axis_index("seq_2")
    far = {"head": 1 - lax.axis_index("head")}
    me = (y * nz + z) * 2 + core
    count = 2 * ny * nz
    rows, width = patches_ref.shape
    cols = q_sc.shape[1]

    def seat(index):
        return {"seq_0": index // (2 * nz), "seq_1": lax.rem(index // 2, nz), "seq_2": lax.rem(index, 2)}

    after, before = seat(lax.rem(me + 1, count)), seat(lax.rem(me + count - 1, count))
    loads = [pltpu.make_async_copy(qkv_hbm.at[j], qkv_w.at[j], weight_sem.at[j]) for j in (1, 2, 0)]
    loads.append(pltpu.make_async_copy(proj_hbm, proj_w, weight_sem.at[3]))
    loads.append(pltpu.make_async_copy(wv_hbm, wv, weight_sem.at[4]))
    for load in loads:
        load.start()
    text_loc = pltpu.make_async_copy(text_ref, text_out.at[me], loc_sem.at[0])
    text_loc.start()
    place = (y, z, ny, nz)
    texts = [Gather(text_ref, text_out, 64, ts, tr, place, c) for c in (0, 1)]
    sights = [Gather(vis_own, vis_out, vis_own.shape[0] // 2, vs, vr, place, c) for c in (0, 1)]

    def on_core(act):
        for c in (0, 1):
            pl.when(core == c)(functools.partial(act, c))

    def pump(count):
        on_core(lambda c: texts[c].advance(count))

    barrier(near(y, z, core, ny, nz) + [after, before, far])
    chunk = rows // 4
    for r in range(0, rows, chunk):
        x = patches_ref[r : r + chunk].astype(f32)
        normed[r : r + chunk] = norm_rows(x, norms_ref[0:1], norms_ref[1:2]).astype(bf16)
    halos = []
    for j, near_ref in ((1, keys), (2, values)):
        loads[j - 1].wait()
        near_ref[1] = jnp.dot(normed[...], qkv_w[j], preferred_element_type=f32).astype(bf16)
        for slot, device in ((0, after), (2, before)):
            number = 2 * (j - 1) + slot // 2
            halos.append(
                pltpu.make_async_remote_copy(
                    src_ref=near_ref.at[1], dst_ref=near_ref.at[slot],
                    send_sem=halo_sem.at[0, number], recv_sem=halo_sem.at[1, number],
                    device_id=device, device_id_type=MESH,
                )
            )
            halos[-1].start()
    on_core(lambda c: texts[c].begin())
    loads[2].wait()
    q_sc[...] = jnp.dot(normed[...], qkv_w[0], preferred_element_type=f32).astype(bf16)
    bias = jnp.where(own_ids_ref[...] == near_ids_ref[...], 0.0, NEG)
    pump(2)
    for halo in halos:
        halo.wait()
    scale = math.log2(math.e) / math.sqrt(VIT_HD)
    for h in range(cols // VIT_HD):
        lo, hi = h * VIT_HD, (h + 1) * VIT_HD
        t0, t1 = lo // 128 * 128, -(-hi // 128) * 128
        lane = lax.broadcasted_iota(jnp.int32, (rows, t1 - t0), 1) + t0
        mine = (lane >= lo) & (lane < hi)
        q = jnp.where(mine, q_sc[:, t0:t1].astype(f32), 0.0).astype(bf16)
        k = keys[:, :, t0:t1].reshape(3 * rows, t1 - t0)
        s = lax.dot_general(q, k, (((1,), (1,)), ((), ())), preferred_element_type=f32) * scale + bias
        e = jnp.exp2(s - jnp.max(s, axis=1, keepdims=True))
        p = (e / jnp.sum(e, axis=1, keepdims=True)).astype(bf16)
        v = values[:, :, t0:t1].reshape(3 * rows, t1 - t0)
        o = jnp.dot(p, v, preferred_element_type=f32)
        if lo == t0:
            mixed[:, t0:t1] = o
        else:
            old = mixed[:, t0:t1] if t1 - t0 == 128 else jnp.concatenate([mixed[:, t0 : t0 + 128], o[:, 128:]], axis=1)
            mixed[:, t0:t1] = jnp.where(mine, o, old)
        pump(2)
    loads[3].wait()
    halves = []
    half = rows // 2
    for i in (0, 1):
        part = slice(i * half, (i + 1) * half)
        part_own[part] = jnp.dot(mixed[part].astype(bf16), proj_w[...], preferred_element_type=f32).astype(bf16)
        halves.append(
            pltpu.make_async_remote_copy(
                src_ref=part_own.at[part], dst_ref=part_far.at[part],
                send_sem=far_sem.at[0, i], recv_sem=far_sem.at[1, i], device_id=far, device_id_type=MESH,
            )
        )
        halves[-1].start()
        pump(2)
    for i in (0, 1):
        pump(4)
        halves[i].wait()
        for r in range(i * half, (i + 1) * half, chunk):
            summed = part_own[r : r + chunk].astype(f32) + part_far[r : r + chunk].astype(f32)
            x = (patches_ref[r : r + chunk].astype(f32) + summed + norms_ref[2:3]).astype(bf16)
            x = norm_rows(x.astype(f32), norms_ref[3:4], norms_ref[4:5])
            for t in range(width // 128):
                merged[t, r : r + chunk] = x[:, t * 128 : (t + 1) * 128]
    loads[4].wait()
    tokens = rows // 4
    total = jnp.zeros((tokens, wv.shape[1]), f32)
    for j in range(4):
        row = [merged[t, pl.ds(j, tokens, stride=4), :] for t in range(width // 128)]
        row = jnp.concatenate(row, axis=1).astype(bf16)
        total = total + jnp.dot(row, wv[j * width : (j + 1) * width], preferred_element_type=f32)
    vis_own[...] = total.astype(bf16)
    vis_loc = pltpu.make_async_copy(vis_own, vis_out.at[me], loc_sem.at[1])
    vis_loc.start()

    def close(c):
        sights[c].begin()
        for _ in sights[c].plan:
            sights[c].advance(1)
            texts[c].advance(1)
        texts[c].finish()
        sights[c].finish()

    on_core(close)
    text_loc.wait()
    vis_loc.wait()


def encode(text, patches, norms, own_ids, near_ids, qkv, proj, wv, ny, nz):
    n = ny * nz * 2
    rows, width = patches.shape
    cols = qkv.shape[2]
    tokens = rows // 4
    bf16, f32 = jnp.bfloat16, jnp.float32
    hbm = pl.BlockSpec(memory_space=pl.ANY)
    vmem = pl.BlockSpec(memory_space=pltpu.VMEM)
    dma = pltpu.SemaphoreType.DMA
    return pl.pallas_call(
        functools.partial(encode_kernel, ny=ny, nz=nz),
        in_specs=[vmem] * 5 + [hbm] * 3,
        out_specs=[hbm, hbm, vmem],
        out_shape=[
            jax.ShapeDtypeStruct((n, *text.shape), bf16),
            jax.ShapeDtypeStruct((n, tokens, wv.shape[1]), bf16),
            jax.ShapeDtypeStruct((tokens, wv.shape[1]), bf16),
        ],
        scratch_shapes=[
            pltpu.VMEM(qkv.shape, bf16), pltpu.VMEM(proj.shape, bf16), pltpu.VMEM(wv.shape, bf16),
            pltpu.VMEM((rows, width), bf16), pltpu.VMEM((rows, cols), bf16),
            pltpu.VMEM((3, rows, cols), bf16), pltpu.VMEM((3, rows, cols), bf16),
            pltpu.VMEM((rows, cols), f32), pltpu.VMEM((rows, width), bf16), pltpu.VMEM((rows, width), bf16),
            pltpu.VMEM((width // 128, rows, 128), f32),
            dma((5,)), dma((2, 4)), dma((2, 2)),
            dma((2 * n + 16,)), dma((n, 2)), dma((2 * n + 16,)), dma((n, 2)), dma((2,)),
        ],
        compiler_params=pltpu.CompilerParams(collective_id=1, has_side_effects=True, vmem_limit_bytes=60 << 20),
        name="encode",
    )(text, patches, norms, own_ids, near_ids, qkv, proj, wv)


def per_device(
    patches, ln_gain, ln_bias, qkv_weight, proj_weight, proj_bias, merge_gain, merge_bias, visual_kv_weight,
    image_tokens, text_before, text_order, queries, text_kv,
):
    seq_index = lax.axis_index(SEQ)
    ny, nz = lax.axis_size("seq_0"), lax.axis_size("seq_1")
    patch_rows = patches.shape[0]
    merged_rows = patch_rows // 4
    total_patches = patch_rows * lax.axis_size(SEQ)
    token_ends = jnp.cumsum(image_tokens)
    near_index = seq_index * patch_rows - patch_rows + jnp.arange(3 * patch_rows, dtype=jnp.int32)
    near_ids = jnp.sum((near_index[:, None] >= 4 * token_ends[None, :]).astype(jnp.int32), axis=1)
    near_ids = jnp.where((near_index >= 0) & (near_index < total_patches), near_ids, -1)
    own_ids = near_ids[patch_rows : 2 * patch_rows]
    text_pos = text_order + jnp.sum(
        jnp.where(text_before[None, :] <= text_order[:, None], image_tokens[None, :], 0), axis=1
    )
    image_starts = token_ends - image_tokens
    steps_before = text_before - jnp.concatenate([jnp.zeros((1,), jnp.int32), text_before[:-1]])
    tokens = queries.shape[0]
    rank = jnp.sum((text_order[None, :] < text_order[:, None]).astype(jnp.int32), axis=1)
    hot = (rank[None, :] == jnp.arange(tokens, dtype=jnp.int32)[:, None]).astype(jnp.bfloat16)
    q = jnp.dot(hot, queries, preferred_element_type=jnp.float32).astype(jnp.bfloat16)
    places = jnp.stack([text_pos // 128, text_pos % 128]).astype(jnp.bfloat16)
    places = lax.dot_general(places, hot, (((1,), (1,)), ((), ())), preferred_element_type=jnp.float32)
    kv = jnp.dot(hot, text_kv.reshape(tokens, -1), preferred_element_type=jnp.float32).astype(jnp.bfloat16)
    places_rows = jnp.pad(places.astype(jnp.bfloat16), ((0, 6), (0, kv.shape[1] - tokens)))
    norms = jnp.stack([ln_gain, ln_bias, proj_bias, merge_gain, merge_bias])
    all_text, all_vis, visual_kv = encode(
        jnp.concatenate([kv, places_rows], axis=0), patches, norms, own_ids[:, None], near_ids[None, :],
        jnp.transpose(qkv_weight, (1, 0, 2)), proj_weight,
        visual_kv_weight.reshape(visual_kv_weight.shape[0], -1), ny, nz,
    )
    visual_kv = visual_kv.reshape(merged_rows, 2, -1)
    key_pos = all_text[:, tokens : tokens + 2, :tokens].astype(jnp.int32)
    key_pos = key_pos[:, 0] * 128 + key_pos[:, 1]
    sources = key_pos.shape[0]
    blocks = sources * tokens // 1024
    key_pos = key_pos.reshape(sources, blocks, tokens // blocks).transpose(1, 0, 2).reshape(blocks, 1024)
    visual_index = jnp.arange(sources * merged_rows, dtype=jnp.int32)
    all_vis_pos = visual_index + jnp.sum(
        jnp.where(image_starts[None, :] <= visual_index[:, None], steps_before[None, :], 0), axis=1
    )
    kp = jnp.concatenate([key_pos, all_vis_pos.reshape(-1, 1024), jnp.full((1, 1024), BIG, jnp.int32)], axis=0)
    places = places.astype(jnp.int32)
    q_pos = (places[0] * 128 + places[1])[:, None]
    attended = attend(q, all_text, all_vis, q_pos, kp, hot.T)
    return (attended, visual_kv)


def solution(mesh):
    split = Mesh(
        mesh.devices.reshape(mesh.shape["grp"], 4, 8, 2, mesh.shape["head"]),
        ("grp", "seq_0", "seq_1", "seq_2", "head"),
    )
    in_specs = (
        P(GRP_SEQ, None),
        P(),
        P(),
        P(None, None, "head"),
        P("head", None),
        P(),
        P(),
        P(),
        P(None, None, "head"),
        P("grp"),
        P("grp"),
        P(GRP_SEQ),
        P(GRP_SEQ, "head"),
        P(GRP_SEQ, None, "head"),
    )
    out_specs = (P(GRP_SEQ, "head"), P(GRP_SEQ, None, "head"))
    return jax.shard_map(
        per_device, mesh=split, in_specs=in_specs, out_specs=out_specs, check_vma=False
    )
```

```python
import functools
import heapq
import math

import jax
import jax.numpy as jnp
from jax import lax
from jax.experimental import pallas as pl
from jax.experimental.pallas import tpu as pltpu
from jax.sharding import Mesh
from jax.sharding import PartitionSpec as P

MESH = pl.DeviceIdType.MESH


VIT_HD = 80
HEAD_DIM = 128
GROUP = 8
SEQ = ("seq_0", "seq_1", "seq_2")
GRP_SEQ = ("grp", "seq_0", "seq_1", "seq_2")


epsilon = 1e-06
NEG = -1e30
SCALE = math.log2(math.e) / math.sqrt(HEAD_DIM)
BIG = 2**30


def attend_kernel(
    q_ref, text_ref, vis_ref, qpos_ref, kp_ref, perm_ref, out_ref,
    kbuf, vbuf, s_sc, x_sc, p_sc, a_sc, o_sc, m_sc, srt_sc, sem, *, tile, texts, sights,
):
    f32, bf16 = jnp.float32, jnp.bfloat16
    d = HEAD_DIM
    rows = GROUP * tile
    blocks = texts + sights
    sources = text_ref.shape[0]
    ranks = kbuf.shape[3]
    size = sources * ranks
    tokens = q_ref.shape[0]

    def copies(h, b):
        if b < texts:
            src = text_ref.at[:, b * ranks : (b + 1) * ranks]
        else:
            src = vis_ref.at[b - texts]
        return [
            pltpu.make_async_copy(src.at[:, :, j * 2 * d + h * d : j * 2 * d + (h + 1) * d], buf.at[h, b, :, :, 0:d], sem.at[h, j, b])
            for j, buf in ((0, kbuf), (1, vbuf))
        ]

    order = sorted(range(blocks), key=lambda b: (b + 0.5) / texts if b < texts else (b - texts + 0.4) / sights)
    for h in range(2):
        for b in order:
            for copy in copies(h, b):
                copy.start()
    heads = kp_ref.shape[0]
    kp = jnp.concatenate([kp_ref[...].astype(f32), jnp.zeros((16 - heads, size), f32)], axis=0)
    columns = [jnp.transpose(kp[:, t * d : (t + 1) * d]) for t in range(size // d)]
    qrow = qpos_ref[...].astype(f32)
    for b in range(blocks + 1):
        for t in range(size // d):
            col = jnp.broadcast_to(columns[t][:, b : b + 1], (d, d))
            mask = jnp.where(col <= qrow, 0.0, NEG).astype(bf16)
            for h in range(2):
                kbuf[h, b, t * d // ranks : (t + 1) * d // ranks, :, d:] = mask.reshape(d // ranks, ranks, d)
    ones = jnp.ones((sources, ranks, d), bf16)
    for h in range(2):
        kbuf[h, blocks, :, :, 0:d] = jnp.zeros((sources, ranks, d), bf16)
        for b in range(blocks):
            vbuf[h, b, :, :, d:] = ones
    first = jnp.min(kp_ref[...], axis=1, keepdims=True)
    lane = lax.broadcasted_iota(jnp.int32, (tile, tokens), 1)
    row = lax.broadcasted_iota(jnp.int32, (tile, tokens), 0)
    qall = qpos_ref[...]
    for h in range(2):
        seen_text, seen_vis = 0, texts
        for i in range(tokens // tile):
            qhi = jnp.max(qall[:, i * tile : (i + 1) * tile], axis=1, keepdims=True)
            visible = (first <= qhi).astype(jnp.int32)
            nt = jnp.sum(visible[0:texts])
            nv = jnp.sum(visible[texts:blocks])
            n = nt + nv

            def arrive(b):
                for j, buf in ((0, kbuf), (1, vbuf)):
                    ref = buf.at[h, b, :, :, 0:d]
                    pltpu.make_async_copy(ref, ref, sem.at[h, j, b]).wait()

            pl.loop(seen_text, nt)(arrive)
            pl.loop(seen_vis, texts + nv)(arrive)
            seen_text, seen_vis = nt, texts + nv
            q = jnp.concatenate(
                [q_ref[i * tile : (i + 1) * tile, (h * GROUP + g) * d : (h * GROUP + g + 1) * d] for g in range(GROUP)], axis=0
            )
            own = (lane == row + i * tile).astype(f32).astype(bf16)
            q = jnp.concatenate([q, jnp.concatenate([own] * GROUP, axis=0)], axis=1)

            def block(j):
                return jnp.minimum(jnp.where(j < nt, j, j - nt + texts), blocks - 1)

            def scores(j, slot):
                k = kbuf[h, jnp.where(j < n, block(j), blocks)].reshape(size, 2 * d)
                s = lax.dot_general(q, k, (((1,), (1,)), ((), ())), preferred_element_type=f32)
                s_sc[slot] = s
                x = s[:, 0:d]
                for c in range(1, size // d):
                    x = jnp.maximum(x, s[:, c * d : (c + 1) * d])
                x_sc[slot] = x

            def weigh(slot):
                old = m_sc[:, 0:1]
                new = jnp.maximum(old, jnp.max(x_sc[slot], axis=1, keepdims=True))
                top = new * SCALE
                p_sc[slot] = jnp.exp2(s_sc[slot] * SCALE - top).astype(bf16)
                a_sc[slot] = jnp.broadcast_to(jnp.exp2(old * SCALE - top), (rows, 2 * d))
                m_sc[...] = jnp.broadcast_to(new, m_sc.shape)

            def add(j, slot):
                v = vbuf[h, block(jnp.maximum(j, 0))].reshape(size, 2 * d)
                o_sc[...] = o_sc[...] * a_sc[slot] + jnp.dot(p_sc[slot], v, preferred_element_type=f32)

            m_sc[...] = jnp.full_like(m_sc, NEG)
            o_sc[...] = jnp.zeros_like(o_sc)
            p_sc[1] = jnp.zeros_like(p_sc[1])
            a_sc[1] = jnp.zeros_like(a_sc[1])
            scores(0, 0)

            @pl.loop(0, (n + 1) // 2)
            def _(pair):
                j = pair * 2
                add(j - 1, 1)
                scores(j + 1, 1)
                weigh(0)
                add(j, 0)
                scores(j + 2, 0)
                weigh(1)

            add(((n + 1) // 2) * 2 - 1, 1)
            o = (o_sc[:, 0:d] / o_sc[:, d : 2 * d]).astype(bf16)
            for g in range(GROUP):
                srt_sc[i * tile : (i + 1) * tile, g * d : (g + 1) * d] = o[g * tile : (g + 1) * tile]
        pl.loop(seen_text, texts)(arrive)
        pl.loop(seen_vis, blocks)(arrive)
        width = GROUP * d
        out_ref[:, h * width : (h + 1) * width] = jnp.dot(
            perm_ref[...], srt_sc[...], preferred_element_type=f32
        ).astype(bf16)


def attend(q, text, vis, qpos, kp, perm):
    sources, tokens, size = text.shape[0], q.shape[0], kp.shape[1]
    ranks = size // sources
    texts, sights = sources * tokens // size, vis.shape[0] * vis.shape[1] // size
    blocks = texts + sights
    tile = 32
    rows = GROUP * tile
    d = HEAD_DIM
    vm = pl.BlockSpec(memory_space=pltpu.VMEM)
    hbm = pl.BlockSpec(memory_space=pl.ANY)
    f32, bf16 = jnp.float32, jnp.bfloat16
    return pl.pallas_call(
        functools.partial(attend_kernel, tile=tile, texts=texts, sights=sights),
        in_specs=[vm, hbm, hbm, vm, vm, vm],
        out_specs=vm,
        out_shape=jax.ShapeDtypeStruct(q.shape, bf16),
        scratch_shapes=[
            pltpu.VMEM((2, blocks + 1, sources, ranks, 2 * d), bf16), pltpu.VMEM((2, blocks, sources, ranks, 2 * d), bf16),
            pltpu.VMEM((2, rows, size), f32), pltpu.VMEM((2, rows, d), f32), pltpu.VMEM((2, rows, size), bf16),
            pltpu.VMEM((2, rows, 2 * d), f32), pltpu.VMEM((rows, 2 * d), f32), pltpu.VMEM((rows, d), f32),
            pltpu.VMEM((tokens, GROUP * d), bf16), pltpu.SemaphoreType.DMA((2, 2, blocks)),
        ],
        compiler_params=pltpu.CompilerParams(vmem_limit_bytes=60 << 20),
        name="attend",
    )(q, text, vis.reshape(sights, sources, ranks, vis.shape[2]), qpos, kp, perm)


def ring_plan(na, nb, jumps=None):
    free = {}
    heap = []
    count = [0]
    def send(axis, way, a, b, part, at):
        start = max(at, free.get((axis, way), 0.0))
        end = start + (1.0 if part == 0 else 0.5)
        free[(axis, way)] = end
        count[0] += 1
        heapq.heappush(heap, (end + 0.9, count[0], axis, way, a, b, part))
    def spread(axis, size, way, off, at, a, b):
        nxt = off + 1
        if nxt < size // 2:
            part = 0
        elif nxt == size // 2:
            part = 1 if way == 1 else 2
        else:
            return None
        return part
    def go(axis, size, way, off, at, a, b):
        part = spread(axis, size, way, off, at, a, b)
        if part is not None:
            na_, nb_ = (a + way, b) if axis == "a" else (a, b + way)
            send(axis, way, na_, nb_, part, at)
    def jump(a, at):
        for step in jumps.get(a, ()):
            send("a", 1 if step > 0 else -1, a + step, 0, 0, at + 0.3 * (abs(step) - 1))
    for way in () if jumps else (1, -1):
        go("a", na, way, 0, 0.0, 0, 0)
    if jumps:
        jump(0, 0.0)
    for way in (1, -1):
        go("b", nb, way, 0, 0.0, 0, 0)
    order = []
    halves = {}
    while heap:
        at, _, axis, way, a, b, part = heapq.heappop(heap)
        order.append((axis, way, a, b, part))
        if axis == "a":
            if jumps:
                jump(a, at)
                for w in (1, -1):
                    go("b", nb, w, 0, at, a, b)
            elif part == 0:
                go("a", na, way, abs(a), at, a, b)
                for w in (1, -1):
                    go("b", nb, w, 0, at, a, b)
            else:
                key = abs(a)
                halves[("a", key, b)] = halves.get(("a", key, b), 0) + 1
                if halves[("a", key, b)] == 2:
                    for w in (1, -1):
                        go("b", nb, w, 0, at, na // 2, b)
        else:
            if part == 0:
                go("b", nb, way, abs(b), at, a, b)
    return order

def barrier(devices):
    sem = pltpu.get_barrier_semaphore()
    for device in devices:
        pl.semaphore_signal(sem, inc=1, device_id=device, device_id_type=MESH)
    pl.semaphore_wait(sem, len(devices))


def near(y, z, core, ny, nz):
    return [
        {"seq_0": lax.rem(y + 1, ny)},
        {"seq_0": lax.rem(y + ny - 1, ny)},
        {"seq_1": lax.rem(z + 1, nz)},
        {"seq_1": lax.rem(z + nz - 1, nz)},
        {"seq_2": 1 - core},
    ]


JUMPS = {0: (2, -2, 1, -1), 2: (2, 1), -2: (-1,)}
PUMPS = (1, 1, 1, 2)


class Gather:
    def __init__(self, own, out, cut, send_sem, recv_sem, place, core, jumps=None):
        self.own, self.out, self.rows, self.cut = own, out, own.shape[0], cut
        self.send_sem, self.recv_sem = send_sem, recv_sem
        self.y, self.z, self.ny, self.nz = place
        self.core = core
        self.along_z = core == 0 or jumps is not None
        self.sizes = (self.nz, self.ny) if self.along_z else (self.ny, self.nz)
        self.jumps = jumps
        self.plan = ring_plan(*self.sizes, jumps)
        self.sent = []
        self.halves = {}
        self.next = 0

    def shard(self, core, dz, dy):
        y = lax.rem(self.y - dy + self.ny, self.ny)
        z = lax.rem(self.z - dz + self.nz, self.nz)
        return (y * self.nz + z) * 2 + core

    def source(self, a, b):
        return self.shard(self.core, a, b) if self.along_z else self.shard(self.core, b, a)

    def piece(self, ref, part):
        if part == 0:
            return ref
        return ref.at[0 : self.cut] if part == 1 else ref.at[self.cut : self.rows]

    def copy(self, src, index, part, number, device):
        return pltpu.make_async_remote_copy(
            src_ref=self.piece(src, part),
            dst_ref=self.piece(self.out.at[index], part),
            send_sem=self.send_sem.at[number],
            recv_sem=self.recv_sem.at[index, 1 if part == 2 else 0],
            device_id=device,
            device_id_type=MESH,
        )

    def neighbour(self, axis, way):
        if (axis == "a") == self.along_z:
            return {"seq_1": lax.rem(self.z + way + self.nz, self.nz)}
        return {"seq_0": lax.rem(self.y + way + self.ny, self.ny)}

    def send(self, src, index, part, device):
        self.copy(src, index, part, len(self.sent), device).start()
        self.sent.append(part)

    def partner(self):
        return {"seq_2": 1 - self.core}

    def begin(self):
        index = self.source(0, 0)
        for way in self.jumps[0] if self.jumps else (1, -1):
            self.send(self.own, index, 0, self.neighbour("a", way))
        for way in (1, -1):
            self.send(self.own, index, 0, self.neighbour("b", way))
        self.send(self.own, index, 0, self.partner())

    def wait(self, index, part):
        self.copy(self.own, index, part, 0, self.partner()).wait_recv()

    def step(self, axis, way, a, b, part):
        index = self.source(a, b)
        self.wait(index, part)
        src = self.out.at[index]
        size = self.sizes[0] if axis == "a" else self.sizes[1]
        off = abs(a) if axis == "a" else abs(b)
        done = True
        if axis == "a" and self.jumps:
            for jump in self.jumps.get(a, ()):
                self.send(src, index, 0, self.neighbour("a", jump))
        elif part == 0:
            half = 0 if off + 1 < size // 2 else (1 if way == 1 else 2)
            self.send(src, index, half, self.neighbour(axis, way))
        else:
            key = (axis, off, off if axis == "a" else a)
            self.halves[key] = self.halves.get(key, 0) + 1
            done = self.halves[key] == 2
        if done:
            if axis == "a":
                for onward in (1, -1):
                    self.send(src, index, 0, self.neighbour("b", onward))
            self.send(src, index, 0, self.partner())

    def advance(self, count):
        for event in self.plan[self.next : self.next + count]:
            self.step(*event)
        self.next = min(len(self.plan), self.next + count)

    def finish(self):
        self.advance(len(self.plan))
        for dz in range(self.nz):
            for dy in range(self.ny):
                self.wait(self.shard(1 - self.core, dz, dy), 0)
        for number, part in enumerate(self.sent):
            self.copy(self.own, 0, part, number, self.partner()).wait_send()


def norm_rows(x, gain, bias):
    centre = jnp.mean(x, axis=-1, keepdims=True)
    centred = x - centre
    spread = jnp.mean(centred * centred, axis=-1, keepdims=True)
    return centred * lax.rsqrt(spread + epsilon) * gain + bias


def encode_kernel(
    text_ref, patches_ref, norms_ref, own_ids_ref, near_ids_ref, qkv_hbm, proj_hbm, wv_hbm,
    text_out, vis_out, vis_own,
    qkv_w, proj_w, wv, normed, q_sc, keys, values, mixed, part_own, part_far, merged,
    weight_sem, halo_sem, far_sem, ts, tr, vs, vr, loc_sem, *, ny, nz,
):
    f32, bf16 = jnp.float32, jnp.bfloat16
    y, z, core = lax.axis_index("seq_0"), lax.axis_index("seq_1"), lax.axis_index("seq_2")
    far = {"head": 1 - lax.axis_index("head")}
    me = (y * nz + z) * 2 + core
    count = 2 * ny * nz
    rows, width = patches_ref.shape
    cols = q_sc.shape[1]

    def seat(index):
        return {"seq_0": index // (2 * nz), "seq_1": lax.rem(index // 2, nz), "seq_2": lax.rem(index, 2)}

    after, before = seat(lax.rem(me + 1, count)), seat(lax.rem(me + count - 1, count))
    loads = [pltpu.make_async_copy(qkv_hbm.at[j], qkv_w.at[j], weight_sem.at[j]) for j in (1, 2, 0)]
    loads.append(pltpu.make_async_copy(proj_hbm, proj_w, weight_sem.at[3]))
    loads.append(pltpu.make_async_copy(wv_hbm, wv, weight_sem.at[4]))
    for load in loads:
        load.start()
    text_loc = pltpu.make_async_copy(text_ref, text_out.at[me], loc_sem.at[0])
    text_loc.start()
    place = (y, z, ny, nz)
    texts = [Gather(text_ref, text_out, 64, ts, tr, place, c) for c in (0, 1)]
    sights = [Gather(vis_own, vis_out, vis_own.shape[0] // 2, vs, vr, place, c, JUMPS if nz == 8 else None) for c in (0, 1)]

    def on_core(act):
        for c in (0, 1):
            pl.when(core == c)(functools.partial(act, c))

    def pump(count):
        on_core(lambda c: texts[c].advance(count))

    skips = [{"seq_1": lax.rem(z + jump + nz, nz)} for jump in (2, -2)] if nz == 8 else []
    barrier(near(y, z, core, ny, nz) + skips + [after, before, far])
    chunk = rows // 4
    for r in range(0, rows, chunk):
        x = patches_ref[r : r + chunk].astype(f32)
        normed[r : r + chunk] = norm_rows(x, norms_ref[0:1], norms_ref[1:2]).astype(bf16)
    halos = []
    for j, near_ref in ((1, keys), (2, values)):
        loads[j - 1].wait()
        near_ref[1] = jnp.dot(normed[...], qkv_w[j], preferred_element_type=f32).astype(bf16)
        for slot, device in ((0, after), (2, before)):
            number = 2 * (j - 1) + slot // 2
            halos.append(
                pltpu.make_async_remote_copy(
                    src_ref=near_ref.at[1], dst_ref=near_ref.at[slot],
                    send_sem=halo_sem.at[0, number], recv_sem=halo_sem.at[1, number],
                    device_id=device, device_id_type=MESH,
                )
            )
            halos[-1].start()
    on_core(lambda c: texts[c].begin())
    loads[2].wait()
    q_sc[...] = jnp.dot(normed[...], qkv_w[0], preferred_element_type=f32).astype(bf16)
    bias = jnp.where(own_ids_ref[...] == near_ids_ref[...], 0.0, NEG)
    pump(PUMPS[0])
    for halo in halos:
        halo.wait()
    scale = math.log2(math.e) / math.sqrt(VIT_HD)
    for h in range(cols // VIT_HD):
        lo, hi = h * VIT_HD, (h + 1) * VIT_HD
        t0, t1 = lo // 128 * 128, -(-hi // 128) * 128
        lane = lax.broadcasted_iota(jnp.int32, (rows, t1 - t0), 1) + t0
        mine = (lane >= lo) & (lane < hi)
        q = jnp.where(mine, q_sc[:, t0:t1].astype(f32), 0.0).astype(bf16)
        k = keys[:, :, t0:t1].reshape(3 * rows, t1 - t0)
        s = lax.dot_general(q, k, (((1,), (1,)), ((), ())), preferred_element_type=f32) * scale + bias
        e = jnp.exp2(s - jnp.max(s, axis=1, keepdims=True))
        p = (e / jnp.sum(e, axis=1, keepdims=True)).astype(bf16)
        v = values[:, :, t0:t1].reshape(3 * rows, t1 - t0)
        o = jnp.dot(p, v, preferred_element_type=f32)
        if lo == t0:
            mixed[:, t0:t1] = o
        else:
            old = mixed[:, t0:t1] if t1 - t0 == 128 else jnp.concatenate([mixed[:, t0 : t0 + 128], o[:, 128:]], axis=1)
            mixed[:, t0:t1] = jnp.where(mine, o, old)
        pump(PUMPS[1])
    loads[3].wait()
    halves = []
    half = rows // 2
    for i in (0, 1):
        part = slice(i * half, (i + 1) * half)
        part_own[part] = jnp.dot(mixed[part].astype(bf16), proj_w[...], preferred_element_type=f32).astype(bf16)
        halves.append(
            pltpu.make_async_remote_copy(
                src_ref=part_own.at[part], dst_ref=part_far.at[part],
                send_sem=far_sem.at[0, i], recv_sem=far_sem.at[1, i], device_id=far, device_id_type=MESH,
            )
        )
        halves[-1].start()
        pump(PUMPS[2])
    for i in (0, 1):
        pump(PUMPS[3])
        halves[i].wait()
        for r in range(i * half, (i + 1) * half, chunk):
            summed = part_own[r : r + chunk].astype(f32) + part_far[r : r + chunk].astype(f32)
            x = (patches_ref[r : r + chunk].astype(f32) + summed + norms_ref[2:3]).astype(bf16)
            x = norm_rows(x.astype(f32), norms_ref[3:4], norms_ref[4:5])
            for t in range(width // 128):
                merged[t, r : r + chunk] = x[:, t * 128 : (t + 1) * 128]
    loads[4].wait()
    tokens = rows // 4
    total = jnp.zeros((tokens, wv.shape[1]), f32)
    for j in range(4):
        row = [merged[t, pl.ds(j, tokens, stride=4), :] for t in range(width // 128)]
        row = jnp.concatenate(row, axis=1).astype(bf16)
        total = total + jnp.dot(row, wv[j * width : (j + 1) * width], preferred_element_type=f32)
    vis_own[...] = total.astype(bf16)
    vis_loc = pltpu.make_async_copy(vis_own, vis_out.at[me], loc_sem.at[1])
    vis_loc.start()

    def close(c):
        sights[c].begin()
        for _ in sights[c].plan:
            sights[c].advance(1)
            texts[c].advance(1)
        texts[c].finish()
        sights[c].finish()

    on_core(close)
    text_loc.wait()
    vis_loc.wait()


def encode(text, patches, norms, own_ids, near_ids, qkv, proj, wv, ny, nz):
    n = ny * nz * 2
    rows, width = patches.shape
    cols = qkv.shape[2]
    tokens = rows // 4
    bf16, f32 = jnp.bfloat16, jnp.float32
    hbm = pl.BlockSpec(memory_space=pl.ANY)
    vmem = pl.BlockSpec(memory_space=pltpu.VMEM)
    dma = pltpu.SemaphoreType.DMA
    return pl.pallas_call(
        functools.partial(encode_kernel, ny=ny, nz=nz),
        in_specs=[vmem] * 5 + [hbm] * 3,
        out_specs=[hbm, hbm, vmem],
        out_shape=[
            jax.ShapeDtypeStruct((n, *text.shape), bf16),
            jax.ShapeDtypeStruct((n, tokens, wv.shape[1]), bf16),
            jax.ShapeDtypeStruct((tokens, wv.shape[1]), bf16),
        ],
        scratch_shapes=[
            pltpu.VMEM(qkv.shape, bf16), pltpu.VMEM(proj.shape, bf16), pltpu.VMEM(wv.shape, bf16),
            pltpu.VMEM((rows, width), bf16), pltpu.VMEM((rows, cols), bf16),
            pltpu.VMEM((3, rows, cols), bf16), pltpu.VMEM((3, rows, cols), bf16),
            pltpu.VMEM((rows, cols), f32), pltpu.VMEM((rows, width), bf16), pltpu.VMEM((rows, width), bf16),
            pltpu.VMEM((width // 128, rows, 128), f32),
            dma((5,)), dma((2, 4)), dma((2, 2)),
            dma((2 * n + 16,)), dma((n, 2)), dma((2 * n + 16,)), dma((n, 2)), dma((2,)),
        ],
        compiler_params=pltpu.CompilerParams(collective_id=1, has_side_effects=True, vmem_limit_bytes=60 << 20),
        name="encode",
    )(text, patches, norms, own_ids, near_ids, qkv, proj, wv)


def per_device(
    patches, ln_gain, ln_bias, qkv_weight, proj_weight, proj_bias, merge_gain, merge_bias, visual_kv_weight,
    image_tokens, text_before, text_order, queries, text_kv,
):
    seq_index = lax.axis_index(SEQ)
    ny, nz = lax.axis_size("seq_0"), lax.axis_size("seq_1")
    patch_rows = patches.shape[0]
    merged_rows = patch_rows // 4
    total_patches = patch_rows * lax.axis_size(SEQ)
    token_ends = jnp.cumsum(image_tokens)
    near_index = seq_index * patch_rows - patch_rows + jnp.arange(3 * patch_rows, dtype=jnp.int32)
    near_ids = jnp.sum((near_index[:, None] >= 4 * token_ends[None, :]).astype(jnp.int32), axis=1)
    near_ids = jnp.where((near_index >= 0) & (near_index < total_patches), near_ids, -1)
    own_ids = near_ids[patch_rows : 2 * patch_rows]
    text_pos = text_order + jnp.sum(
        jnp.where(text_before[None, :] <= text_order[:, None], image_tokens[None, :], 0), axis=1
    )
    image_starts = token_ends - image_tokens
    steps_before = text_before - jnp.concatenate([jnp.zeros((1,), jnp.int32), text_before[:-1]])
    tokens = queries.shape[0]
    rank = jnp.sum((text_order[None, :] < text_order[:, None]).astype(jnp.int32), axis=1)
    hot = (rank[None, :] == jnp.arange(tokens, dtype=jnp.int32)[:, None]).astype(jnp.bfloat16)
    q = jnp.dot(hot, queries, preferred_element_type=jnp.float32).astype(jnp.bfloat16)
    places = jnp.stack([text_pos // 128, text_pos % 128]).astype(jnp.bfloat16)
    places = lax.dot_general(places, hot, (((1,), (1,)), ((), ())), preferred_element_type=jnp.float32)
    kv = jnp.dot(hot, text_kv.reshape(tokens, -1), preferred_element_type=jnp.float32).astype(jnp.bfloat16)
    places_rows = jnp.pad(places.astype(jnp.bfloat16), ((0, 6), (0, kv.shape[1] - tokens)))
    norms = jnp.stack([ln_gain, ln_bias, proj_bias, merge_gain, merge_bias])
    all_text, all_vis, visual_kv = encode(
        jnp.concatenate([kv, places_rows], axis=0), patches, norms, own_ids[:, None], near_ids[None, :],
        jnp.transpose(qkv_weight, (1, 0, 2)), proj_weight,
        visual_kv_weight.reshape(visual_kv_weight.shape[0], -1), ny, nz,
    )
    visual_kv = visual_kv.reshape(merged_rows, 2, -1)
    key_pos = all_text[:, tokens : tokens + 2, :tokens].astype(jnp.int32)
    key_pos = key_pos[:, 0] * 128 + key_pos[:, 1]
    sources = key_pos.shape[0]
    blocks = sources * tokens // 1024
    key_pos = key_pos.reshape(sources, blocks, tokens // blocks).transpose(1, 0, 2).reshape(blocks, 1024)
    visual_index = jnp.arange(sources * merged_rows, dtype=jnp.int32)
    all_vis_pos = visual_index + jnp.sum(
        jnp.where(image_starts[None, :] <= visual_index[:, None], steps_before[None, :], 0), axis=1
    )
    kp = jnp.concatenate([key_pos, all_vis_pos.reshape(-1, 1024), jnp.full((1, 1024), BIG, jnp.int32)], axis=0)
    places = places.astype(jnp.int32)
    q_pos = (places[0] * 128 + places[1])[None, :]
    attended = attend(q, all_text, all_vis, q_pos, kp, hot.T)
    return (attended, visual_kv)


def solution(mesh):
    split = Mesh(
        mesh.devices.reshape(mesh.shape["grp"], 4, 8, 2, mesh.shape["head"]),
        ("grp", "seq_0", "seq_1", "seq_2", "head"),
    )
    in_specs = (
        P(GRP_SEQ, None),
        P(),
        P(),
        P(None, None, "head"),
        P("head", None),
        P(),
        P(),
        P(),
        P(None, None, "head"),
        P("grp"),
        P("grp"),
        P(GRP_SEQ),
        P(GRP_SEQ, "head"),
        P(GRP_SEQ, None, "head"),
    )
    out_specs = (P(GRP_SEQ, "head"), P(GRP_SEQ, None, "head"))
    return jax.shard_map(
        per_device, mesh=split, in_specs=in_specs, out_specs=out_specs, check_vma=False
    )
```

```python
import functools
import heapq
import math

import jax
import jax.numpy as jnp
from jax import lax
from jax.experimental import pallas as pl
from jax.experimental.pallas import tpu as pltpu
from jax.sharding import Mesh
from jax.sharding import PartitionSpec as P

MESH = pl.DeviceIdType.MESH


VIT_HD = 80
HEAD_DIM = 128
GROUP = 8
SEQ = ("seq_0", "seq_1", "seq_2")
GRP_SEQ = ("grp", "seq_0", "seq_1", "seq_2")


epsilon = 1e-06
NEG = -1e30
SCALE = math.log2(math.e) / math.sqrt(HEAD_DIM)
BIG = 2**30


def attend_kernel(
    q_ref, text_ref, vis_ref, qpos_ref, kp_ref, perm_ref, out_ref,
    kbuf, vbuf, s_sc, x_sc, p_sc, a_sc, o_sc, m_sc, srt_sc, sem, *, tile, texts, sights,
):
    f32, bf16 = jnp.float32, jnp.bfloat16
    d = HEAD_DIM
    rows = GROUP * tile
    blocks = texts + sights
    sources = text_ref.shape[0]
    ranks = kbuf.shape[3]
    size = sources * ranks
    tokens = q_ref.shape[0]

    def copies(h, b):
        if b < texts:
            src = text_ref.at[:, b * ranks : (b + 1) * ranks]
        else:
            src = vis_ref.at[b - texts]
        return [
            pltpu.make_async_copy(src.at[:, :, j * 2 * d + h * d : j * 2 * d + (h + 1) * d], buf.at[h, b, :, :, 0:d], sem.at[h, j, b])
            for j, buf in ((0, kbuf), (1, vbuf))
        ]

    order = sorted(range(blocks), key=lambda b: (b + 0.5) / texts if b < texts else (b - texts + 0.4) / sights)
    for h in range(2):
        for b in order:
            for copy in copies(h, b):
                copy.start()
    heads = kp_ref.shape[0]
    kp = jnp.concatenate([kp_ref[...].astype(f32), jnp.zeros((16 - heads, size), f32)], axis=0)
    columns = [jnp.transpose(kp[:, t * d : (t + 1) * d]) for t in range(size // d)]
    qrow = qpos_ref[...].astype(f32)
    for b in range(blocks + 1):
        for t in range(size // d):
            col = jnp.broadcast_to(columns[t][:, b : b + 1], (d, d))
            mask = jnp.where(col <= qrow, 0.0, NEG).astype(bf16)
            for h in range(2):
                kbuf[h, b, t * d // ranks : (t + 1) * d // ranks, :, d:] = mask.reshape(d // ranks, ranks, d)
    ones = jnp.ones((sources, ranks, d), bf16)
    for h in range(2):
        kbuf[h, blocks, :, :, 0:d] = jnp.zeros((sources, ranks, d), bf16)
        for b in range(blocks):
            vbuf[h, b, :, :, d:] = ones
    first = jnp.min(kp_ref[...], axis=1, keepdims=True)
    lane = lax.broadcasted_iota(jnp.int32, (tile, tokens), 1)
    row = lax.broadcasted_iota(jnp.int32, (tile, tokens), 0)
    qall = qpos_ref[...]
    for h in range(2):
        seen_text, seen_vis = 0, texts
        for i in range(tokens // tile):
            qhi = jnp.max(qall[:, i * tile : (i + 1) * tile], axis=1, keepdims=True)
            visible = (first <= qhi).astype(jnp.int32)
            nt = jnp.sum(visible[0:texts])
            nv = jnp.sum(visible[texts:blocks])
            n = nt + nv

            def arrive(b):
                for j, buf in ((0, kbuf), (1, vbuf)):
                    ref = buf.at[h, b, :, :, 0:d]
                    pltpu.make_async_copy(ref, ref, sem.at[h, j, b]).wait()

            pl.loop(seen_text, nt)(arrive)
            pl.loop(seen_vis, texts + nv)(arrive)
            seen_text, seen_vis = nt, texts + nv
            q = jnp.concatenate(
                [q_ref[i * tile : (i + 1) * tile, (h * GROUP + g) * d : (h * GROUP + g + 1) * d] for g in range(GROUP)], axis=0
            )
            own = (lane == row + i * tile).astype(f32).astype(bf16)
            q = jnp.concatenate([q, jnp.concatenate([own] * GROUP, axis=0)], axis=1)

            def block(j):
                return jnp.minimum(jnp.where(j < nt, j, j - nt + texts), blocks - 1)

            def scores(j, slot):
                k = kbuf[h, jnp.where(j < n, block(j), blocks)].reshape(size, 2 * d)
                s = lax.dot_general(q, k, (((1,), (1,)), ((), ())), preferred_element_type=f32)
                s_sc[slot] = s
                x = s[:, 0:d]
                for c in range(1, size // d):
                    x = jnp.maximum(x, s[:, c * d : (c + 1) * d])
                x_sc[slot] = x

            def weigh(slot):
                old = m_sc[:, 0:1]
                new = jnp.maximum(old, jnp.max(x_sc[slot], axis=1, keepdims=True))
                top = new * SCALE
                p_sc[slot] = jnp.exp2(s_sc[slot] * SCALE - top).astype(bf16)
                a_sc[slot] = jnp.broadcast_to(jnp.exp2(old * SCALE - top), (rows, 2 * d))
                m_sc[...] = jnp.broadcast_to(new, m_sc.shape)

            def add(j, slot):
                v = vbuf[h, block(jnp.maximum(j, 0))].reshape(size, 2 * d)
                o_sc[...] = o_sc[...] * a_sc[slot] + jnp.dot(p_sc[slot], v, preferred_element_type=f32)

            m_sc[...] = jnp.full_like(m_sc, NEG)
            o_sc[...] = jnp.zeros_like(o_sc)
            p_sc[1] = jnp.zeros_like(p_sc[1])
            a_sc[1] = jnp.zeros_like(a_sc[1])
            scores(0, 0)

            @pl.loop(0, (n + 1) // 2)
            def _(pair):
                j = pair * 2
                add(j - 1, 1)
                scores(j + 1, 1)
                weigh(0)
                add(j, 0)
                scores(j + 2, 0)
                weigh(1)

            add(((n + 1) // 2) * 2 - 1, 1)
            o = (o_sc[:, 0:d] / o_sc[:, d : 2 * d]).astype(bf16)
            for g in range(GROUP):
                srt_sc[i * tile : (i + 1) * tile, g * d : (g + 1) * d] = o[g * tile : (g + 1) * tile]
        pl.loop(seen_text, texts)(arrive)
        pl.loop(seen_vis, blocks)(arrive)
        width = GROUP * d
        out_ref[:, h * width : (h + 1) * width] = jnp.dot(
            perm_ref[...], srt_sc[...], preferred_element_type=f32
        ).astype(bf16)


def attend(q, text, vis, qpos, kp, perm):
    sources, tokens, size = text.shape[0], q.shape[0], kp.shape[1]
    ranks = size // sources
    texts, sights = sources * tokens // size, vis.shape[0] * vis.shape[1] // size
    blocks = texts + sights
    tile = 32
    rows = GROUP * tile
    d = HEAD_DIM
    vm = pl.BlockSpec(memory_space=pltpu.VMEM)
    hbm = pl.BlockSpec(memory_space=pl.ANY)
    f32, bf16 = jnp.float32, jnp.bfloat16
    return pl.pallas_call(
        functools.partial(attend_kernel, tile=tile, texts=texts, sights=sights),
        in_specs=[vm, hbm, hbm, vm, vm, vm],
        out_specs=vm,
        out_shape=jax.ShapeDtypeStruct(q.shape, bf16),
        scratch_shapes=[
            pltpu.VMEM((2, blocks + 1, sources, ranks, 2 * d), bf16), pltpu.VMEM((2, blocks, sources, ranks, 2 * d), bf16),
            pltpu.VMEM((2, rows, size), f32), pltpu.VMEM((2, rows, d), f32), pltpu.VMEM((2, rows, size), bf16),
            pltpu.VMEM((2, rows, 2 * d), f32), pltpu.VMEM((rows, 2 * d), f32), pltpu.VMEM((rows, d), f32),
            pltpu.VMEM((tokens, GROUP * d), bf16), pltpu.SemaphoreType.DMA((2, 2, blocks)),
        ],
        compiler_params=pltpu.CompilerParams(vmem_limit_bytes=60 << 20),
        name="attend",
    )(q, text, vis.reshape(sights, sources, ranks, vis.shape[2]), qpos, kp, perm)


def ring_plan(na, nb, jumps=None):
    free = {}
    heap = []
    count = [0]
    def send(axis, way, a, b, part, at):
        start = max(at, free.get((axis, way), 0.0))
        end = start + (1.0 if part == 0 else 0.5)
        free[(axis, way)] = end
        count[0] += 1
        heapq.heappush(heap, (end + 0.9, count[0], axis, way, a, b, part))
    def spread(axis, size, way, off, at, a, b):
        nxt = off + 1
        if nxt < size // 2:
            part = 0
        elif nxt == size // 2:
            part = 1 if way == 1 else 2
        else:
            return None
        return part
    def go(axis, size, way, off, at, a, b):
        part = spread(axis, size, way, off, at, a, b)
        if part is not None:
            na_, nb_ = (a + way, b) if axis == "a" else (a, b + way)
            send(axis, way, na_, nb_, part, at)
    def jump(a, at):
        for step in jumps.get(a, ()):
            send("a", 1 if step > 0 else -1, a + step, 0, 0, at + 0.3 * (abs(step) - 1))
    for way in () if jumps else (1, -1):
        go("a", na, way, 0, 0.0, 0, 0)
    if jumps:
        jump(0, 0.0)
    for way in (1, -1):
        go("b", nb, way, 0, 0.0, 0, 0)
    order = []
    halves = {}
    while heap:
        at, _, axis, way, a, b, part = heapq.heappop(heap)
        order.append((axis, way, a, b, part))
        if axis == "a":
            if jumps:
                jump(a, at)
                for w in (1, -1):
                    go("b", nb, w, 0, at, a, b)
            elif part == 0:
                go("a", na, way, abs(a), at, a, b)
                for w in (1, -1):
                    go("b", nb, w, 0, at, a, b)
            else:
                key = abs(a)
                halves[("a", key, b)] = halves.get(("a", key, b), 0) + 1
                if halves[("a", key, b)] == 2:
                    for w in (1, -1):
                        go("b", nb, w, 0, at, na // 2, b)
        else:
            if part == 0:
                go("b", nb, way, abs(b), at, a, b)
    return order

def barrier(devices):
    sem = pltpu.get_barrier_semaphore()
    for device in devices:
        pl.semaphore_signal(sem, inc=1, device_id=device, device_id_type=MESH)
    pl.semaphore_wait(sem, len(devices))


def near(y, z, core, ny, nz):
    return [
        {"seq_0": lax.rem(y + 1, ny)},
        {"seq_0": lax.rem(y + ny - 1, ny)},
        {"seq_1": lax.rem(z + 1, nz)},
        {"seq_1": lax.rem(z + nz - 1, nz)},
        {"seq_2": 1 - core},
    ]


JUMPS = {0: (2, -2, 1, -1), 2: (2, 1), -2: (-1,)}
PUMPS = (1, 1, 1, 2)


class Gather:
    def __init__(self, own, out, cut, send_sem, recv_sem, place, core, jumps=None):
        self.own, self.out, self.rows, self.cut = own, out, own.shape[0], cut
        self.send_sem, self.recv_sem = send_sem, recv_sem
        self.y, self.z, self.ny, self.nz = place
        self.core = core
        self.along_z = core == 0 or jumps is not None
        self.sizes = (self.nz, self.ny) if self.along_z else (self.ny, self.nz)
        self.jumps = jumps
        self.plan = ring_plan(*self.sizes, jumps)
        self.sent = []
        self.halves = {}
        self.next = 0

    def shard(self, core, dz, dy):
        y = lax.rem(self.y - dy + self.ny, self.ny)
        z = lax.rem(self.z - dz + self.nz, self.nz)
        return (y * self.nz + z) * 2 + core

    def source(self, a, b):
        return self.shard(self.core, a, b) if self.along_z else self.shard(self.core, b, a)

    def piece(self, ref, part):
        if part == 0:
            return ref
        return ref.at[0 : self.cut] if part == 1 else ref.at[self.cut : self.rows]

    def copy(self, src, index, part, number, device):
        return pltpu.make_async_remote_copy(
            src_ref=self.piece(src, part),
            dst_ref=self.piece(self.out.at[index], part),
            send_sem=self.send_sem.at[number],
            recv_sem=self.recv_sem.at[index, 1 if part == 2 else 0],
            device_id=device,
            device_id_type=MESH,
        )

    def neighbour(self, axis, way):
        if (axis == "a") == self.along_z:
            return {"seq_1": lax.rem(self.z + way + self.nz, self.nz)}
        return {"seq_0": lax.rem(self.y + way + self.ny, self.ny)}

    def send(self, src, index, part, device):
        self.copy(src, index, part, len(self.sent), device).start()
        self.sent.append(part)

    def partner(self):
        return {"seq_2": 1 - self.core}

    def begin(self):
        index = self.source(0, 0)
        for way in self.jumps[0] if self.jumps else (1, -1):
            self.send(self.own, index, 0, self.neighbour("a", way))
        for way in (1, -1):
            self.send(self.own, index, 0, self.neighbour("b", way))
        self.send(self.own, index, 0, self.partner())

    def wait(self, index, part):
        self.copy(self.own, index, part, 0, self.partner()).wait_recv()

    def step(self, axis, way, a, b, part):
        index = self.source(a, b)
        self.wait(index, part)
        src = self.out.at[index]
        size = self.sizes[0] if axis == "a" else self.sizes[1]
        off = abs(a) if axis == "a" else abs(b)
        done = True
        if axis == "a" and self.jumps:
            for jump in self.jumps.get(a, ()):
                self.send(src, index, 0, self.neighbour("a", jump))
        elif part == 0:
            half = 0 if off + 1 < size // 2 else (1 if way == 1 else 2)
            self.send(src, index, half, self.neighbour(axis, way))
        else:
            key = (axis, off, off if axis == "a" else a)
            self.halves[key] = self.halves.get(key, 0) + 1
            done = self.halves[key] == 2
        if done:
            if axis == "a":
                for onward in (1, -1):
                    self.send(src, index, 0, self.neighbour("b", onward))
            self.send(src, index, 0, self.partner())

    def advance(self, count):
        for event in self.plan[self.next : self.next + count]:
            self.step(*event)
        self.next = min(len(self.plan), self.next + count)

    def finish(self):
        self.advance(len(self.plan))
        for dz in range(self.nz):
            for dy in range(self.ny):
                self.wait(self.shard(1 - self.core, dz, dy), 0)
        for number, part in enumerate(self.sent):
            self.copy(self.own, 0, part, number, self.partner()).wait_send()


def norm_rows(x, gain, bias):
    centre = jnp.mean(x, axis=-1, keepdims=True)
    centred = x - centre
    spread = jnp.mean(centred * centred, axis=-1, keepdims=True)
    return centred * lax.rsqrt(spread + epsilon) * gain + bias


def encode_kernel(
    text_ref, patches_ref, norms_ref, own_ids_ref, near_ids_ref, qkv_hbm, proj_hbm, wv_hbm,
    text_out, vis_out, vis_own,
    qkv_w, proj_w, wv, normed, q_sc, keys, values, mixed, mixed_own, mixed_far, proj_far, summed, merged,
    weight_sem, halo_sem, far_sem, proj_sem, ts, tr, vs, vr, loc_sem, *, ny, nz,
):
    f32, bf16 = jnp.float32, jnp.bfloat16
    y, z, core = lax.axis_index("seq_0"), lax.axis_index("seq_1"), lax.axis_index("seq_2")
    far = {"head": 1 - lax.axis_index("head")}
    me = (y * nz + z) * 2 + core
    count = 2 * ny * nz
    rows, width = patches_ref.shape
    cols = q_sc.shape[1]

    def seat(index):
        return {"seq_0": index // (2 * nz), "seq_1": lax.rem(index // 2, nz), "seq_2": lax.rem(index, 2)}

    after, before = seat(lax.rem(me + 1, count)), seat(lax.rem(me + count - 1, count))
    loads = [pltpu.make_async_copy(qkv_hbm.at[j], qkv_w.at[j], weight_sem.at[j]) for j in (1, 2, 0)]
    loads.append(pltpu.make_async_copy(proj_hbm, proj_w, weight_sem.at[3]))
    loads.append(pltpu.make_async_copy(wv_hbm, wv, weight_sem.at[4]))
    for load in loads:
        load.start()
    text_loc = pltpu.make_async_copy(text_ref, text_out.at[me], loc_sem.at[0])
    text_loc.start()
    place = (y, z, ny, nz)
    texts = [Gather(text_ref, text_out, 64, ts, tr, place, c) for c in (0, 1)]
    sights = [Gather(vis_own, vis_out, vis_own.shape[0] // 2, vs, vr, place, c, JUMPS if nz == 8 else None) for c in (0, 1)]

    def on_core(act):
        for c in (0, 1):
            pl.when(core == c)(functools.partial(act, c))

    def pump(count):
        on_core(lambda c: texts[c].advance(count))

    skips = [{"seq_1": lax.rem(z + jump + nz, nz)} for jump in (2, -2)] if nz == 8 else []
    barrier(near(y, z, core, ny, nz) + skips + [after, before, far])
    share = proj_hbm.shape[0] // 2
    my_share = pl.ds(pl.multiple_of(core * share, share), share)

    def hand(src, number, device):
        return pltpu.make_async_remote_copy(
            src_ref=src, dst_ref=proj_far.at[my_share],
            send_sem=proj_sem.at[0, number], recv_sem=proj_sem.at[1, number], device_id=device, device_id_type=MESH,
        )

    push = hand(proj_hbm.at[my_share], 0, far)
    push.start()
    forward = hand(proj_far.at[my_share], 1, {"seq_2": 1 - core})
    chunk = rows // 4
    for r in range(0, rows, chunk):
        x = patches_ref[r : r + chunk].astype(f32)
        normed[r : r + chunk] = norm_rows(x, norms_ref[0:1], norms_ref[1:2]).astype(bf16)
    halos = []
    for j, near_ref in ((1, keys), (2, values)):
        loads[j - 1].wait()
        near_ref[1] = jnp.dot(normed[...], qkv_w[j], preferred_element_type=f32).astype(bf16)
        for slot, device in ((0, after), (2, before)):
            number = 2 * (j - 1) + slot // 2
            halos.append(
                pltpu.make_async_remote_copy(
                    src_ref=near_ref.at[1], dst_ref=near_ref.at[slot],
                    send_sem=halo_sem.at[0, number], recv_sem=halo_sem.at[1, number],
                    device_id=device, device_id_type=MESH,
                )
            )
            halos[-1].start()
    on_core(lambda c: texts[c].begin())
    loads[2].wait()
    q_sc[...] = jnp.dot(normed[...], qkv_w[0], preferred_element_type=f32).astype(bf16)
    bias = jnp.where(own_ids_ref[...] == near_ids_ref[...], 0.0, NEG)
    pump(PUMPS[0])
    for halo in halos:
        halo.wait()
    scale = math.log2(math.e) / math.sqrt(VIT_HD)
    tiles = []
    for h in range(cols // VIT_HD):
        lo, hi = h * VIT_HD, (h + 1) * VIT_HD
        t0, t1 = lo // 128 * 128, -(-hi // 128) * 128
        lane = lax.broadcasted_iota(jnp.int32, (rows, t1 - t0), 1) + t0
        mine = (lane >= lo) & (lane < hi)
        q = jnp.where(mine, q_sc[:, t0:t1].astype(f32), 0.0).astype(bf16)
        k = keys[:, :, t0:t1].reshape(3 * rows, t1 - t0)
        s = lax.dot_general(q, k, (((1,), (1,)), ((), ())), preferred_element_type=f32) * scale + bias
        e = jnp.exp2(s - jnp.max(s, axis=1, keepdims=True))
        p = (e / jnp.sum(e, axis=1, keepdims=True)).astype(bf16)
        v = values[:, :, t0:t1].reshape(3 * rows, t1 - t0)
        o = jnp.dot(p, v, preferred_element_type=f32)
        if lo == t0:
            mixed[:, t0:t1] = o
        else:
            old = mixed[:, t0:t1] if t1 - t0 == 128 else jnp.concatenate([mixed[:, t0 : t0 + 128], o[:, 128:]], axis=1)
            mixed[:, t0:t1] = jnp.where(mine, o, old)
        for t in range(len(tiles), hi // 128):
            mixed_own[t] = mixed[:, t * 128 : (t + 1) * 128].astype(bf16)
            tiles.append(
                pltpu.make_async_remote_copy(
                    src_ref=mixed_own.at[t], dst_ref=mixed_far.at[t],
                    send_sem=far_sem.at[0, t], recv_sem=far_sem.at[1, t], device_id=far, device_id_type=MESH,
                )
            )
            tiles[-1].start()
        pump(PUMPS[1])
    push.wait()
    forward.start()
    loads[3].wait()

    def projected(parts, weight):
        return jnp.dot(jnp.concatenate([parts[t] for t in range(cols // 128)], axis=1), weight[...], preferred_element_type=f32)

    summed[...] = projected(mixed_own, proj_w)
    pump(PUMPS[2])
    forward.wait()
    for tile in tiles:
        tile.wait()
    summed[...] = summed[...] + projected(mixed_far, proj_far)
    for r in range(0, rows, chunk):
        x = (patches_ref[r : r + chunk].astype(f32) + summed[r : r + chunk] + norms_ref[2:3]).astype(bf16)
        x = norm_rows(x.astype(f32), norms_ref[3:4], norms_ref[4:5])
        for t in range(width // 128):
            merged[t, r : r + chunk] = x[:, t * 128 : (t + 1) * 128]
    pump(PUMPS[3])
    loads[4].wait()
    tokens = rows // 4
    total = jnp.zeros((tokens, wv.shape[1]), f32)
    for j in range(4):
        row = [merged[t, pl.ds(j, tokens, stride=4), :] for t in range(width // 128)]
        row = jnp.concatenate(row, axis=1).astype(bf16)
        total = total + jnp.dot(row, wv[j * width : (j + 1) * width], preferred_element_type=f32)
    vis_own[...] = total.astype(bf16)
    vis_loc = pltpu.make_async_copy(vis_own, vis_out.at[me], loc_sem.at[1])
    vis_loc.start()

    def close(c):
        sights[c].begin()
        for _ in sights[c].plan:
            sights[c].advance(1)
            texts[c].advance(1)
        texts[c].finish()
        sights[c].finish()

    on_core(close)
    text_loc.wait()
    vis_loc.wait()


def encode(text, patches, norms, own_ids, near_ids, qkv, proj, wv, ny, nz):
    n = ny * nz * 2
    rows, width = patches.shape
    cols = qkv.shape[2]
    tokens = rows // 4
    bf16, f32 = jnp.bfloat16, jnp.float32
    hbm = pl.BlockSpec(memory_space=pl.ANY)
    vmem = pl.BlockSpec(memory_space=pltpu.VMEM)
    dma = pltpu.SemaphoreType.DMA
    return pl.pallas_call(
        functools.partial(encode_kernel, ny=ny, nz=nz),
        in_specs=[vmem] * 5 + [hbm] * 3,
        out_specs=[hbm, hbm, vmem],
        out_shape=[
            jax.ShapeDtypeStruct((n, *text.shape), bf16),
            jax.ShapeDtypeStruct((n, tokens, wv.shape[1]), bf16),
            jax.ShapeDtypeStruct((tokens, wv.shape[1]), bf16),
        ],
        scratch_shapes=[
            pltpu.VMEM(qkv.shape, bf16), pltpu.VMEM(proj.shape, bf16), pltpu.VMEM(wv.shape, bf16),
            pltpu.VMEM((rows, width), bf16), pltpu.VMEM((rows, cols), bf16),
            pltpu.VMEM((3, rows, cols), bf16), pltpu.VMEM((3, rows, cols), bf16),
            pltpu.VMEM((rows, cols), f32), pltpu.VMEM((cols // 128, rows, 128), bf16),
            pltpu.VMEM((cols // 128, rows, 128), bf16), pltpu.VMEM(proj.shape, bf16), pltpu.VMEM((rows, width), f32),
            pltpu.VMEM((width // 128, rows, 128), f32),
            dma((5,)), dma((2, 4)), dma((2, cols // 128)), dma((2, 2)),
            dma((2 * n + 16,)), dma((n, 2)), dma((2 * n + 16,)), dma((n, 2)), dma((2,)),
        ],
        compiler_params=pltpu.CompilerParams(collective_id=1, has_side_effects=True, vmem_limit_bytes=60 << 20),
        name="encode",
    )(text, patches, norms, own_ids, near_ids, qkv, proj, wv)


def per_device(
    patches, ln_gain, ln_bias, qkv_weight, proj_weight, proj_bias, merge_gain, merge_bias, visual_kv_weight,
    image_tokens, text_before, text_order, queries, text_kv,
):
    seq_index = lax.axis_index(SEQ)
    ny, nz = lax.axis_size("seq_0"), lax.axis_size("seq_1")
    patch_rows = patches.shape[0]
    merged_rows = patch_rows // 4
    total_patches = patch_rows * lax.axis_size(SEQ)
    token_ends = jnp.cumsum(image_tokens)
    near_index = seq_index * patch_rows - patch_rows + jnp.arange(3 * patch_rows, dtype=jnp.int32)
    near_ids = jnp.sum((near_index[:, None] >= 4 * token_ends[None, :]).astype(jnp.int32), axis=1)
    near_ids = jnp.where((near_index >= 0) & (near_index < total_patches), near_ids, -1)
    own_ids = near_ids[patch_rows : 2 * patch_rows]
    text_pos = text_order + jnp.sum(
        jnp.where(text_before[None, :] <= text_order[:, None], image_tokens[None, :], 0), axis=1
    )
    image_starts = token_ends - image_tokens
    steps_before = text_before - jnp.concatenate([jnp.zeros((1,), jnp.int32), text_before[:-1]])
    tokens = queries.shape[0]
    rank = jnp.sum((text_order[None, :] < text_order[:, None]).astype(jnp.int32), axis=1)
    hot = (rank[None, :] == jnp.arange(tokens, dtype=jnp.int32)[:, None]).astype(jnp.bfloat16)
    q = jnp.dot(hot, queries, preferred_element_type=jnp.float32).astype(jnp.bfloat16)
    places = jnp.stack([text_pos // 128, text_pos % 128]).astype(jnp.bfloat16)
    places = lax.dot_general(places, hot, (((1,), (1,)), ((), ())), preferred_element_type=jnp.float32)
    kv = jnp.dot(hot, text_kv.reshape(tokens, -1), preferred_element_type=jnp.float32).astype(jnp.bfloat16)
    places_rows = jnp.pad(places.astype(jnp.bfloat16), ((0, 6), (0, kv.shape[1] - tokens)))
    norms = jnp.stack([ln_gain, ln_bias, proj_bias, merge_gain, merge_bias])
    all_text, all_vis, visual_kv = encode(
        jnp.concatenate([kv, places_rows], axis=0), patches, norms, own_ids[:, None], near_ids[None, :],
        jnp.transpose(qkv_weight, (1, 0, 2)), proj_weight,
        visual_kv_weight.reshape(visual_kv_weight.shape[0], -1), ny, nz,
    )
    visual_kv = visual_kv.reshape(merged_rows, 2, -1)
    key_pos = all_text[:, tokens : tokens + 2, :tokens].astype(jnp.int32)
    key_pos = key_pos[:, 0] * 128 + key_pos[:, 1]
    sources = key_pos.shape[0]
    blocks = sources * tokens // 1024
    key_pos = key_pos.reshape(sources, blocks, tokens // blocks).transpose(1, 0, 2).reshape(blocks, 1024)
    visual_index = jnp.arange(sources * merged_rows, dtype=jnp.int32)
    all_vis_pos = visual_index + jnp.sum(
        jnp.where(image_starts[None, :] <= visual_index[:, None], steps_before[None, :], 0), axis=1
    )
    kp = jnp.concatenate([key_pos, all_vis_pos.reshape(-1, 1024), jnp.full((1, 1024), BIG, jnp.int32)], axis=0)
    places = places.astype(jnp.int32)
    q_pos = (places[0] * 128 + places[1])[None, :]
    attended = attend(q, all_text, all_vis, q_pos, kp, hot.T)
    return (attended, visual_kv)


def solution(mesh):
    split = Mesh(
        mesh.devices.reshape(mesh.shape["grp"], 4, 8, 2, mesh.shape["head"]),
        ("grp", "seq_0", "seq_1", "seq_2", "head"),
    )
    in_specs = (
        P(GRP_SEQ, None),
        P(),
        P(),
        P(None, None, "head"),
        P("head", None),
        P(),
        P(),
        P(),
        P(None, None, "head"),
        P("grp"),
        P("grp"),
        P(GRP_SEQ),
        P(GRP_SEQ, "head"),
        P(GRP_SEQ, None, "head"),
    )
    out_specs = (P(GRP_SEQ, "head"), P(GRP_SEQ, None, "head"))
    return jax.shard_map(
        per_device, mesh=split, in_specs=in_specs, out_specs=out_specs, check_vma=False
    )
```
